256 devices in a mesh: pix: 32 (over y, x, core), site: 8 (over z).
Axes of the slice: x: 4, y: 4, z: 8, core: 2. Of those that a mesh axis runs over, the one named last changes fastest.
Arguments:
- margins: int32 [2048, 256, 1024], P('pix', None, 'site'), may hold values from -2047 to 2047
- block_pos: int32 [2048, 8], P('pix', 'site'), may hold values from -1 to 15, as said below
- pattern_ids: int32 [1024], P('site'), may hold values from 0 to 15
- pattern_gain: float32 [16, 256], replicated, may hold values from -4 to 4
- site_price: float32 [1024], P('site'), may hold values from 0.2 to 4
- weights: float32 [131072], P('pix'), may hold values from 0.2 to 2
- site_start: float32 [1024], P('site'), may hold values from 0 to 1
- pixel_start: float32 [131072], P('pix'), may hold values from 0 to 1
- dual_start: float32 [131072], P('pix'), may hold values from 0 to 2
Outputs:
- site_level: float32 [1024], P('site')
- pixel_level: float32 [131072], P('pix')
- duals: float32 [131072], P('pix')
The draws below stay inside these ranges and needn't reach their ends.
Inputs may be any that keep to these rules, and one draw needn't show every extreme that they name: Row k of block_pos and of margins is held by pixel device k // 64 and belongs to pixel device (k // 2) % 32; its entry for site block b is the position, among that device's 16 pixel blocks, of the pixel block of the tile, or -1 for an empty slot. The lists are filled unevenly. For one pixel device, drawn afresh, every slot that belongs to it is filled in every row group and site block.
All inputs are finite; a program needn't handle non-finite values.
Results may differ from the reference program's by a relative error of at most 0.0003.
Values may be sent and summed in bfloat16 or wider, within the bound.
No kernel may reach another device: no remote copies, remote signals or barrier semaphores. Data moves between devices by JAX's collectives and lax.ppermute only.
A program may use at most 64 MiB of HBM per device.

```python
import math
import jax
import jax.numpy as jnp
from jax import lax

PB_DEV = 16
PIXB = 256
SITEB = 128
CAP = 2
NPAT = 16
ITERS = 2
PIXELS = 131072
SITES = 1024
SLOTS = 2048
N_PIX = 32
N_SITE = 8


def draw_block_pos(key, part):
    key = jax.random.fold_in(key, 4099)
    key_roll, key_pos, key_star = jax.random.split(key, 3)
    slot = jnp.arange(SLOTS, dtype=jnp.int32)[:, None]
    column = jnp.arange(N_SITE, dtype=jnp.int32)[None, :]
    per_source = N_PIX * CAP
    source = slot // per_source
    target = slot % per_source // CAP
    within = slot % CAP
    pix_span = max(N_PIX - 1, 1)
    site_span = max(N_SITE - 1, 1)
    denom = 2 * pix_span * site_span
    roll = jax.random.randint(key_roll, (SLOTS, N_SITE), 0, 10 * denom, dtype=jnp.int32)
    filled = roll < 3 * denom + 3 * ((source + target) * site_span + 2 * column * pix_span)
    chosen = jax.random.randint(key_star, (), 0, N_PIX, dtype=jnp.int32)
    filled = filled | (target == chosen)
    position = jax.random.randint(key_pos, (SLOTS, N_SITE), 0, PB_DEV, dtype=jnp.int32)
    result = jnp.where(filled, position, -1)
    leading = (source == 0) & (within == 0) & (column == 0)
    result = jnp.where(leading & (target == chosen), PB_DEV - 1, result)
    result = jnp.where(leading & (target == (chosen + 1) % N_PIX), -1, result)
    return result.astype(jnp.int32)


def set_ends(array, key, smallest, top_value):
    spot = [jax.random.randint(jax.random.fold_in(key, axis), (), 0, length) for axis, length in enumerate(array.shape)]
    longest = array.shape.index(max(array.shape))
    next_to = spot[:longest] + [(spot[longest] + 1) % array.shape[longest]] + spot[longest + 1:]
    return array.at[tuple(spot)].set(smallest).at[tuple(next_to)].set(top_value)


def block_levels(stream_key, extent, cuts, low, high):
    factor_of = 1.0
    for dim, parts in cuts:
        steps = jax.random.uniform(jax.random.fold_in(jax.random.fold_in(stream_key, 6), dim), (parts,), jnp.float32, low / len(cuts), high / len(cuts))
        factor_of = factor_of * jnp.repeat(jnp.exp(steps), extent[dim] // parts).reshape((-1,) + (1,) * (len(extent) - 1 - dim))
    return factor_of


def centred(rng, extent, scale, most, held_as=jnp.bfloat16):
    values = jax.random.normal(rng, extent, jnp.float32) * scale
    return jnp.minimum(jnp.maximum(values, -most), most).astype(held_as)


def setup_inputs(seed: int = 0) -> dict:
    streams_of = jax.random.split(jax.random.key(seed), 10)
    return {
        "margins": set_ends(jax.random.randint(streams_of[0], (SLOTS, PIXB, SITES), -2047, 2048), jax.random.fold_in(streams_of[0], 1), -2047, 2047).astype(jnp.int32),
        "block_pos": draw_block_pos(jax.random.fold_in(streams_of[9], 71), 0),
        "pattern_ids": set_ends(jax.random.randint(streams_of[2], (SITES,), 0, NPAT), jax.random.fold_in(streams_of[2], 1), 0, NPAT - 1).astype(jnp.int32),
        "pattern_gain": centred(streams_of[3], (NPAT, PIXB), 1.0, 4.0, jnp.float32),
        "site_price": jnp.clip(jnp.exp(math.log(4.0) - 2.9957323 * jax.random.uniform(streams_of[4], (SITES,), jnp.float32) ** block_levels(streams_of[4], (SITES,), ((0, 8),), -0.2, 0.2)), 0.2, 4.0),
        "weights": jnp.clip(jnp.exp(math.log(2.0) - 2.3025851 * jax.random.uniform(streams_of[5], (PIXELS,), jnp.float32) ** block_levels(streams_of[5], (PIXELS,), ((0, 32),), -0.2, 0.2)), 0.2, 2.0),
        "site_start": jnp.clip(1.0 * jax.random.uniform(streams_of[6], (SITES,), jnp.float32) ** block_levels(streams_of[6], (SITES,), ((0, 8),), -0.2, 0.2), 0.0, 1.0),
        "pixel_start": jnp.clip(1.0 * jax.random.uniform(streams_of[7], (PIXELS,), jnp.float32) ** block_levels(streams_of[7], (PIXELS,), ((0, 32),), -0.2, 0.2), 0.0, 1.0),
        "dual_start": jnp.clip(2.0 * jax.random.uniform(streams_of[8], (PIXELS,), jnp.float32) ** block_levels(streams_of[8], (PIXELS,), ((0, 32),), -0.2, 0.2), 0.0, 2.0),
    }


MARGIN_SCALE = 2.0 ** -9


def build_tiles(margin_rows, positions, gain_tile):
    filled = jnp.repeat(positions >= 0, SITEB, axis=1)
    values = jax.nn.sigmoid(margin_rows.astype(jnp.float32) * MARGIN_SCALE + gain_tile[None])
    return jnp.where(filled[:, None, :], values, 0.0).astype(jnp.bfloat16)


def block_index(positions):
    target = jnp.arange(N_PIX * CAP, dtype=jnp.int32) // CAP
    return jnp.where(positions >= 0, target[:, None] * PB_DEV + positions, 0).astype(jnp.int32)


def apply_transpose(margin_groups, position_groups, gain_tile, dual_half):
    def absorb(running, pieces):
        margin_rows, positions = pieces
        coverage = build_tiles(margin_rows, positions, gain_tile).astype(jnp.float32)
        coverage = coverage.reshape(coverage.shape[0], PIXB, N_SITE, SITEB)
        picked = dual_half[block_index(positions)].astype(jnp.float32)
        partial_value = jnp.einsum("kbr,krbj->bj", picked, coverage, precision=lax.Precision.HIGHEST)
        return running + partial_value.reshape(SITES), None

    running, unused = lax.scan(absorb, jnp.zeros((SITES,), jnp.float32), (margin_groups, position_groups))
    return running


def apply_forward(margin_groups, position_groups, gain_tile, site_half):
    spread = site_half.astype(jnp.float32).reshape(N_SITE, SITEB)

    def absorb(running, pieces):
        margin_rows, positions = pieces
        coverage = build_tiles(margin_rows, positions, gain_tile).astype(jnp.float32)
        coverage = coverage.reshape(coverage.shape[0], PIXB, N_SITE, SITEB)
        products = jnp.einsum("krbj,bj->kbr", coverage, spread, precision=lax.Precision.HIGHEST)
        running = running.at[block_index(positions).reshape(-1)].add(products.reshape(-1, PIXB))
        return running, None

    running, unused = lax.scan(absorb, jnp.zeros((PB_DEV * N_PIX, PIXB), jnp.float32), (margin_groups, position_groups))
    return running.reshape(PIXELS)


def reference(margins, block_pos, pattern_ids, pattern_gain, site_price, weights, site_start, pixel_start, dual_start):
    gain_tile = pattern_gain[pattern_ids].T
    margin_groups = margins.reshape(N_PIX, N_PIX * CAP, PIXB, SITES)
    position_groups = block_pos.reshape(N_PIX, N_PIX * CAP, N_SITE)
    ones_pixels = jnp.ones((PB_DEV * N_PIX, PIXB), jnp.bfloat16)
    column_sum = apply_transpose(margin_groups, position_groups, gain_tile, ones_pixels)
    row_sum = apply_forward(margin_groups, position_groups, gain_tile, jnp.ones((SITES,), jnp.bfloat16))
    site_level, pixel_level, duals = site_start, pixel_start, dual_start
    for iteration in range(ITERS):
        dual_half = duals.astype(jnp.bfloat16).reshape(PB_DEV * N_PIX, PIXB)
        pulled = apply_transpose(margin_groups, position_groups, gain_tile, dual_half)
        new_site = jnp.clip(site_level - (site_price - pulled / column_sum), 0.0, 1.0)
        new_pixel = jnp.clip(pixel_level - (duals - weights), 0.0, 1.0)
        extrapolated = (2.0 * new_site - site_level).astype(jnp.bfloat16)
        pushed = apply_forward(margin_groups, position_groups, gain_tile, extrapolated)
        duals = jnp.maximum(duals + ((2.0 * new_pixel - pixel_level) - pushed) / (row_sum + 1.0), 0.0)
        site_level, pixel_level = new_site, new_pixel
    return site_level, pixel_level, duals
```

```python
import functools

import jax
import jax.numpy as jnp
from jax import lax
from jax.experimental import pallas as pl
from jax.experimental.pallas import tpu as pltpu
from jax.sharding import PartitionSpec as P

F32 = jnp.float32
BF16 = jnp.bfloat16
HALF_SCALE = 2.0 ** (-10)
VMEM = pl.BlockSpec(memory_space=pltpu.VMEM)


def iota(shape, dim):
    return lax.broadcasted_iota(jnp.int32, shape, dim)


def dot(a, b, dims=((1,), (0,))):
    return lax.dot_general(a, b, (dims, ((), ())), preferred_element_type=F32)


def exact_pick(onehot, values, dims):
    high = values.astype(BF16)
    rest = values - high.astype(F32)
    middle = rest.astype(BF16)
    low = (rest - middle.astype(F32)).astype(BF16)
    return dot(onehot, high, dims) + (dot(onehot, middle, dims) + dot(onehot, low, dims))


def call(body, outs, *args, scratch=(), specs=None, flops=0, nbytes=0):
    return pl.pallas_call(
        body,
        out_shape=[jax.ShapeDtypeStruct(s, d) for s, d in outs],
        in_specs=specs or [VMEM] * len(args),
        out_specs=[VMEM] * len(outs),
        scratch_shapes=list(scratch),
        cost_estimate=pl.CostEstimate(flops=flops, transcendentals=0, bytes_accessed=nbytes),
        compiler_params=pltpu.CompilerParams(vmem_limit_bytes=48 * 1024 * 1024),
    )(*args)


def build_kernel(chunks, m_hbm, pos_ref, ids_ref, gain_ref, cov_ref, sum_ref, map_ref, buf, half_gain, sems):
    slots = m_hbm.shape[0]
    per = slots // chunks
    copies = []
    for c in range(chunks):
        part = pl.ds(c * per, per)
        copy = pltpu.make_async_copy(m_hbm.at[part], buf.at[part], sems.at[c])
        copy.start()
        copies.append(copy)
    patterns = gain_ref.shape[0]
    onehot = (ids_ref[...] == iota((patterns, 128), 0)).astype(BF16)
    half_gain[...] = 0.5 * gain_pick(gain_ref[...], onehot)
    rows = 4 * slots
    expand = (iota((rows, slots), 1) == (iota((rows, slots), 0) >> 2)).astype(BF16)
    wide = jnp.broadcast_to(pos_ref[...].astype(F32), (slots, 128)).astype(BF16)
    map_ref[...] = dot(expand, wide)
    sum_ref[...] = jnp.zeros_like(sum_ref)
    for c in range(chunks):
        copies[c].wait()

        def pair(t, carry):
            marks = map_ref[pl.ds(pl.multiple_of(t * 8, 8), 8), :]
            total = jnp.zeros((8, 128), F32)
            for i in range(2):
                level = buf[2 * t + i].astype(F32) * HALF_SCALE + half_gain[...]
                tile = (0.5 * jnp.tanh(level) + 0.5).astype(BF16)
                cov_ref[t, :, i * 128 : (i + 1) * 128] = tile
                part = jnp.sum(tile.astype(F32).reshape(-1, 8, 128), axis=0)
                total = total + jnp.where(marks[4 * i : 4 * i + 1] >= 0.0, part, 0.0)
            sum_ref[...] += total
            return carry

        lax.fori_loop(c * per // 2, (c + 1) * per // 2, pair, 0)


def gain_pick(gain, onehot):
    dims = ((0,), (0,))
    high = gain.astype(BF16)
    rest = gain - high.astype(F32)
    middle = rest.astype(BF16)
    low = (rest - middle.astype(F32)).astype(BF16)
    return dot(high, onehot, dims) + (dot(middle, onehot, dims) + dot(low, onehot, dims))


def pull(x_ref, cov_ref):
    first = (iota((8, 128), 0) & 2) == 0
    total = jnp.zeros((8, 256), F32)
    for t in range(cov_ref.shape[0]):
        x = x_ref[t * 8 : (t + 1) * 8, :]
        left = jnp.concatenate([jnp.where(first, x, 0.0), jnp.where(first, 0.0, x)], axis=1)
        total = total + dot(left.astype(BF16), cov_ref[t])
    own = jnp.where(iota((8, 128), 0) < 4, total[:, :128], total[:, 128:])
    return jnp.sum(own, axis=0, keepdims=True)


def push(row, plain, cov_ref, out_ref):
    spot = iota((8, 128), 0)
    value = jnp.broadcast_to(row, (8, 128))
    if plain:
        value = jnp.where((spot & 1) == 1, value, 1.0)
    left = jnp.concatenate([jnp.where(spot < 4, value, 0.0), jnp.where(spot < 4, 0.0, value)], axis=1).astype(BF16)
    first = (spot & 2) == 0
    for t in range(cov_ref.shape[0]):
        product = dot(left, cov_ref[t], ((1,), (1,)))
        out_ref[t * 8 : (t + 1) * 8, :] = jnp.where(first, product[:, :128], product[:, 128:])


def positions(marks):
    tiles = marks.reshape(-1, 8, 128)
    spot = iota(tiles.shape, 1)
    return jnp.where(spot < 2, tiles[:, 2:3, :], tiles).reshape(marks.shape)


def kinds(rows):
    spot = iota((rows, 128), 0)
    return (spot & 1).astype(F32), ((spot >> 1) & 1).astype(F32)


def first_pull_kernel(ag_ref, map_ref, cov_ref, sum_ref, out_ref, x_ref):
    rows = map_ref.shape[0]
    marks = map_ref[...]
    q, h = kinds(rows)
    tile = (iota((rows, 128), 0) >> 3).astype(F32)
    key = jnp.where((marks >= 0.0) & (q == 0.0), tile * 32.0 + marks * 2.0 + h, -1.0)
    picked = jnp.zeros((rows, 128), F32)
    for c in range(ag_ref.shape[0] // 128):
        lane = (iota((rows, 128), 1) + c * 128).astype(F32)
        picked = picked + dot((lane == key).astype(BF16), ag_ref[c * 128 : (c + 1) * 128, :])
    x_ref[...] = picked
    pulled = pull(x_ref, cov_ref)
    sums = jnp.sum(sum_ref[...], axis=0, keepdims=True)
    tiles = marks.reshape(-1, 8, 128)
    spot = iota(tiles.shape, 1)
    out_ref[...] = jnp.where(spot == 0, sums[None], jnp.where(spot == 1, pulled[None], tiles)).reshape(rows, 128)


def first_push_kernel(in_ref, price_ref, site_ref, cov_ref, out_ref, new_ref, sum_ref):
    totals = jnp.sum(in_ref[...].reshape(-1, 8, 128), axis=0)
    column_sum = totals[0:1]
    new = jnp.clip(site_ref[...] - (price_ref[...] - totals[1:2] / column_sum), 0.0, 1.0)
    new_ref[...] = new
    sum_ref[...] = column_sum
    push(2.0 * new - site_ref[...], True, cov_ref, out_ref)


def first_spread_kernel(x_ref, marks_ref, out_ref):
    rows = x_ref.shape[0]
    marks = positions(marks_ref[...])
    q, h = kinds(rows)
    key = jnp.where(marks >= 0.0, q * 32.0 + marks * 2.0 + h, -1.0)
    onehot = (iota((rows, 128), 1).astype(F32) == key).astype(BF16)[:, :64]
    spread = exact_pick(onehot, x_ref[...], ((0,), (0,)))
    for s in range(out_ref.shape[0]):
        out_ref[s] = spread


def step(pixel, dual, weight, pushed, row_sum):
    new = jnp.clip(pixel - (dual - weight), 0.0, 1.0)
    return new, jnp.maximum(dual + ((2.0 * new - pixel) - pushed) / (row_sum + 1.0), 0.0)


def first_dual_kernel(in_ref, marks_ref, dual_ref, weight_ref, pixel_ref, out_ref, new_dual_ref, new_pixel_ref, row_ref):
    totals = jnp.sum(in_ref[...], axis=0)
    row_sum = totals[:32]
    row_ref[...] = row_sum
    new_pixel, new_dual = step(pixel_ref[...], dual_ref[...], weight_ref[...], totals[32:], row_sum)
    new_pixel_ref[...] = new_pixel
    new_dual_ref[...] = new_dual
    rows = marks_ref.shape[0]
    marks = positions(marks_ref[...])
    q, h = kinds(rows)
    key = jnp.where((marks >= 0.0) & (q == 0.0), marks * 2.0 + h, -1.0)
    onehot = (iota((rows, 128), 1).astype(F32) == key).astype(BF16)[:, :32]
    out_ref[...] = dot(onehot, new_dual.astype(BF16))


def pull_kernel(x_ref, cov_ref, out_ref):
    out_ref[...] = jnp.broadcast_to(pull(x_ref, cov_ref), out_ref.shape)


def push_kernel(in_ref, price_ref, site_ref, sum_ref, cov_ref, out_ref, new_ref):
    totals = jnp.sum(in_ref[...].reshape(-1, 8, 128), axis=0)
    new = jnp.clip(site_ref[...] - (price_ref[...] - totals[0:1] / sum_ref[...]), 0.0, 1.0)
    new_ref[...] = new
    push(2.0 * new - site_ref[...], False, cov_ref, out_ref)


def spread_kernel(x_ref, marks_ref, out_ref):
    rows = x_ref.shape[0]
    marks = positions(marks_ref[...])
    q, h = kinds(rows)
    key = jnp.where((marks >= 0.0) & (q == 0.0), marks * 2.0 + h, -1.0)
    onehot = (iota((rows, 128), 1).astype(F32) == key).astype(BF16)[:, :32]
    spread = exact_pick(onehot, x_ref[...], ((0,), (0,)))
    for s in range(out_ref.shape[0]):
        out_ref[s] = spread


def dual_kernel(in_ref, row_ref, dual_ref, weight_ref, pixel_ref, new_dual_ref, new_pixel_ref):
    pushed = jnp.sum(in_ref[...], axis=0)
    new_pixel_ref[...], new_dual_ref[...] = step(
        pixel_ref[...], dual_ref[...], weight_ref[...], pushed, row_ref[...]
    )


def local(
    n_pix,
    n_site,
    margins,
    block_pos,
    pattern_ids,
    pattern_gain,
    site_price,
    weights,
    site_start,
    pixel_start,
    dual_start,
):
    slots = margins.shape[0]
    rows = 4 * slots
    chunks = 16
    to_pix = lambda x: lax.all_to_all(x.reshape(n_pix, -1, 128), "pix", 0, 0, tiled=True).reshape(-1, 128)
    to_site = lambda x: lax.all_to_all(x, "site", 0, 0, tiled=True)
    price, site0 = site_price.reshape(1, 128), site_start.reshape(1, 128)
    dual0, weight, pixel0 = (v.reshape(32, 128) for v in (dual_start, weights, pixel_start))

    copies = jnp.broadcast_to(dual0.astype(BF16)[None], (n_pix, 32, 128))
    gathered = to_pix(copies)
    hbm = pl.BlockSpec(memory_space=pl.ANY)
    cov, sums, marks = call(
        functools.partial(build_kernel, chunks),
        [((slots // 2, 256, 256), BF16), ((8, 128), F32), ((rows, 128), F32)],
        margins,
        block_pos,
        pattern_ids.reshape(1, 128),
        pattern_gain,
        scratch=[
            pltpu.VMEM(margins.shape, jnp.int32),
            pltpu.VMEM((256, 128), F32),
            pltpu.SemaphoreType.DMA((chunks,)),
        ],
        specs=[hbm, VMEM, VMEM, VMEM],
        flops=10 * margins.size,
        nbytes=6 * margins.size,
    )
    message = ((rows, 128), F32)
    (out,) = call(first_pull_kernel, [message], gathered, marks, cov, sums, scratch=[pltpu.VMEM((rows, 128), F32)])
    summed = to_pix(out)
    out, site1, column_sum = call(
        first_push_kernel, [message, ((1, 128), F32), ((1, 128), F32)], summed, price, site0, cov
    )
    (out,) = call(first_spread_kernel, [((n_site, 64, 128), F32)], to_pix(out), summed)
    out, dual1, pixel1, row_sum = call(
        first_dual_kernel, [message] + [((32, 128), F32)] * 3, to_site(out), summed, dual0, weight, pixel0
    )
    (out,) = call(pull_kernel, [message], to_pix(out), cov)
    out, site2 = call(push_kernel, [message, ((1, 128), F32)], to_pix(out), price, site1, column_sum, cov)
    (out,) = call(spread_kernel, [((n_site, 32, 128), F32)], to_pix(out), summed)
    dual2, pixel2 = call(dual_kernel, [((32, 128), F32)] * 2, to_site(out), row_sum, dual1, weight, pixel1)
    return site2.reshape(-1), pixel2.reshape(-1), dual2.reshape(-1)


def solution(mesh):
    placed = (
        P("pix", None, "site"),
        P("pix", "site"),
        P("site"),
        P(),
        P("site"),
        P("pix"),
        P("site"),
        P("pix"),
        P("pix"),
    )
    return jax.shard_map(
        functools.partial(local, mesh.shape["pix"], mesh.shape["site"]),
        mesh=mesh,
        in_specs=placed,
        out_specs=(P("site"), P("pix"), P("pix")),
        check_vma=False,
    )
```

```python
import functools

import jax
import jax.numpy as jnp
from jax import lax
from jax.experimental import pallas as pl
from jax.experimental.pallas import tpu as pltpu
from jax.sharding import PartitionSpec as P

F32 = jnp.float32
BF16 = jnp.bfloat16
HALF_SCALE = 2.0 ** (-10)
VMEM = pl.BlockSpec(memory_space=pltpu.VMEM)
HBM = pl.BlockSpec(memory_space=pltpu.HBM)


def iota(shape, dim):
    return lax.broadcasted_iota(jnp.int32, shape, dim)


def dot(a, b, dims=((1,), (0,))):
    return lax.dot_general(a, b, (dims, ((), ())), preferred_element_type=F32)


def exact_pick(onehot, values, dims):
    high = values.astype(BF16)
    rest = values - high.astype(F32)
    middle = rest.astype(BF16)
    low = (rest - middle.astype(F32)).astype(BF16)
    return dot(onehot, high, dims) + (dot(onehot, middle, dims) + dot(onehot, low, dims))


def call(body, outs, *args, scratch=(), specs=None, flops=0, nbytes=0, mib=8):
    return pl.pallas_call(
        body,
        out_shape=[o if hasattr(o, "memory_space") else jax.ShapeDtypeStruct(*o) for o in outs],
        in_specs=specs or [VMEM] * len(args),
        out_specs=[HBM if hasattr(o, "memory_space") else VMEM for o in outs],
        scratch_shapes=list(scratch),
        cost_estimate=pl.CostEstimate(flops=flops, transcendentals=0, bytes_accessed=nbytes),
        compiler_params=pltpu.CompilerParams(vmem_limit_bytes=mib * 1024 * 1024),
    )(*args)


def in_hbm(value):
    return pltpu.with_memory_space_constraint(value, pltpu.HBM)


def prepare_kernel(dual_hbm, out_ref, dual_ref, sem):
    copy = pltpu.make_async_copy(dual_hbm, dual_ref, sem)
    copy.start()
    copy.wait()
    dual = dual_ref[...].astype(BF16)
    for t in range(out_ref.shape[0]):
        out_ref[t] = dual


def build_kernel(
    chunks,
    m_hbm,
    pos_hbm,
    ids_hbm,
    gain_hbm,
    near_ref,
    far_hbm,
    sum_ref,
    map_ref,
    pick_ref,
    buf,
    far_ref,
    half_gain,
    pos_ref,
    ids_ref,
    gain_ref,
    sems,
    small_sems,
    far_sems,
):
    small = [(pos_hbm, pos_ref), (ids_hbm, ids_ref), (gain_hbm, gain_ref)]
    small = [pltpu.make_async_copy(src, dst, small_sems.at[n]) for n, (src, dst) in enumerate(small)]
    for copy in small:
        copy.start()
    slots = m_hbm.shape[0]
    per = slots // chunks
    copies = {}
    for c in reversed(range(chunks)):
        part = pl.ds(c * per, per)
        copy = pltpu.make_async_copy(m_hbm.at[part], buf.at[part], sems.at[c])
        copy.start()
        copies[c] = copy
    for copy in small:
        copy.wait()
    patterns = gain_ref.shape[0]
    onehot = (ids_ref[...] == iota((patterns, 128), 0)).astype(BF16)
    half_gain[...] = 0.5 * gain_pick(gain_ref[...], onehot)
    rows = 4 * slots
    expand = (iota((rows, slots), 1) == (iota((rows, slots), 0) >> 2)).astype(BF16)
    wide = jnp.broadcast_to(pos_ref[...].astype(F32), (128, slots)).astype(BF16)
    marks = dot(expand, wide, ((1,), (1,)))
    map_ref[...] = marks
    q, h = kinds(rows)
    tile = (iota((rows, 128), 0) >> 3).astype(F32)
    key = jnp.where((marks >= 0.0) & (q == 0.0), tile * 32.0 + marks * 2.0 + h, -1.0)
    for c in range(pick_ref.shape[1] // 128):
        lane = (iota((rows, 128), 1) + c * 128).astype(F32)
        pick_ref[:, c * 128 : (c + 1) * 128] = (lane == key).astype(BF16)
    sum_ref[...] = jnp.zeros_like(sum_ref)
    near = near_ref.shape[0]
    sent = []

    def pairs(first, last, out_ref, offset):
        def pair(t, carry):
            marks = map_ref[pl.ds(pl.multiple_of(t * 8, 8), 8), :]
            total = jnp.zeros((8, 128), F32)
            for i in range(2):
                level = buf[2 * t + i].astype(F32) * HALF_SCALE + half_gain[...]
                tile = (0.5 * jnp.tanh(level) + 0.5).astype(BF16)
                out_ref[t - offset, :, i * 128 : (i + 1) * 128] = tile
                part = jnp.sum(tile.astype(F32).reshape(-1, 8, 128), axis=0)
                total = total + jnp.where(marks[4 * i : 4 * i + 1] >= 0.0, part, 0.0)
            sum_ref[...] += total
            return carry

        lax.fori_loop(first, last, pair, 0)

    for c in reversed(range(chunks)):
        copies[c].wait()
        first, last = c * per // 2, (c + 1) * per // 2
        if first >= near:
            pairs(first, last, far_ref, near)
            part = pl.ds(first - near, last - first)
            copy = pltpu.make_async_copy(far_ref.at[part], far_hbm.at[part], far_sems.at[c])
            copy.start()
            sent.append(copy)
        else:
            pairs(first, last, near_ref, 0)
    for copy in sent:
        copy.wait()


def gain_pick(gain, onehot):
    dims = ((0,), (0,))
    high = gain.astype(BF16)
    rest = gain - high.astype(F32)
    middle = rest.astype(BF16)
    low = (rest - middle.astype(F32)).astype(BF16)
    return dot(high, onehot, dims) + (dot(middle, onehot, dims) + dot(low, onehot, dims))


def tiles(*refs):
    return [ref.at[t] for ref in refs for t in range(ref.shape[0])]


def pull(x_ref, cov):
    first = (iota((8, 128), 0) & 2) == 0
    total = jnp.zeros((8, 256), F32)
    for t, tile in enumerate(cov):
        x = x_ref[t * 8 : (t + 1) * 8, :]
        left = jnp.concatenate([jnp.where(first, x, 0.0), jnp.where(first, 0.0, x)], axis=1)
        total = total + dot(left.astype(BF16), tile[...])
    own = jnp.where(iota((8, 128), 0) < 4, total[:, :128], total[:, 128:])
    return jnp.sum(own, axis=0, keepdims=True)


def push(row, plain, cov, out_ref):
    spot = iota((8, 128), 0)
    value = jnp.broadcast_to(row, (8, 128))
    if plain:
        value = jnp.where((spot & 1) == 1, value, 1.0)
    left = jnp.concatenate([jnp.where(spot < 4, value, 0.0), jnp.where(spot < 4, 0.0, value)], axis=1).astype(BF16)
    first = (spot & 2) == 0
    for t, tile in enumerate(cov):
        product = dot(left, tile[...], ((1,), (1,)))
        out_ref[t * 8 : (t + 1) * 8, :] = jnp.where(first, product[:, :128], product[:, 128:])


def positions(marks):
    tiles = marks.reshape(-1, 8, 128)
    spot = iota(tiles.shape, 1)
    return jnp.where(spot < 2, tiles[:, 2:3, :], tiles).reshape(marks.shape)


def kinds(rows):
    spot = iota((rows, 128), 0)
    return (spot & 1).astype(F32), ((spot >> 1) & 1).astype(F32)


def first_pull_kernel(ag_ref, pick_ref, map_ref, near_ref, far_hbm, sum_ref, out_ref, far_ref, x_ref, sem):
    copy = pltpu.make_async_copy(far_hbm, far_ref, sem)
    copy.start()
    x_ref[...] = dot(pick_ref[...], ag_ref[...])
    near = near_ref.shape[0]
    pulled = pull(x_ref, tiles(near_ref))
    copy.wait()
    pulled = pulled + pull(x_ref.at[near * 8 :], tiles(far_ref))
    sums = jnp.sum(sum_ref[...], axis=0, keepdims=True)
    marks = map_ref[...].reshape(-1, 8, 128)
    spot = iota(marks.shape, 1)
    out = jnp.where(spot == 0, sums[None], jnp.where(spot == 1, pulled[None], marks))
    out_ref[...] = out.reshape(out_ref.shape)


def first_push_kernel(in_ref, price_ref, site_ref, near_ref, far_ref, out_ref, new_ref, sum_ref):
    totals = jnp.sum(in_ref[...].reshape(-1, 8, 128), axis=0)
    column_sum = totals[0:1]
    new = jnp.clip(site_ref[...] - (price_ref[...] - totals[1:2] / column_sum), 0.0, 1.0)
    new_ref[...] = new
    sum_ref[...] = column_sum
    push(2.0 * new - site_ref[...], True, tiles(near_ref, far_ref), out_ref)


def first_spread_kernel(x_ref, marks_ref, out_ref):
    rows = x_ref.shape[0]
    marks = positions(marks_ref[...])
    q, h = kinds(rows)
    key = jnp.where(marks >= 0.0, q * 32.0 + marks * 2.0 + h, -1.0)
    onehot = (iota((rows, 128), 1).astype(F32) == key).astype(BF16)[:, :64]
    spread = exact_pick(onehot, x_ref[...], ((0,), (0,)))
    for s in range(out_ref.shape[0]):
        out_ref[s] = spread


def step(pixel, dual, weight, pushed, row_sum):
    new = jnp.clip(pixel - (dual - weight), 0.0, 1.0)
    return new, jnp.maximum(dual + ((2.0 * new - pixel) - pushed) / (row_sum + 1.0), 0.0)


def first_dual_kernel(in_ref, marks_ref, dual_ref, weight_ref, pixel_ref, out_ref, new_dual_ref, new_pixel_ref, row_ref):
    totals = jnp.sum(in_ref[...], axis=0)
    row_sum = totals[:32]
    row_ref[...] = row_sum
    new_pixel, new_dual = step(pixel_ref[...], dual_ref[...], weight_ref[...], totals[32:], row_sum)
    new_pixel_ref[...] = new_pixel
    new_dual_ref[...] = new_dual
    rows = marks_ref.shape[0]
    marks = positions(marks_ref[...])
    q, h = kinds(rows)
    key = jnp.where((marks >= 0.0) & (q == 0.0), marks * 2.0 + h, -1.0)
    onehot = (iota((rows, 128), 1).astype(F32) == key).astype(BF16)[:, :32]
    out_ref[...] = dot(onehot, new_dual.astype(BF16))


def pull_kernel(x_ref, near_ref, far_ref, out_ref):
    out_ref[...] = jnp.broadcast_to(pull(x_ref, tiles(near_ref, far_ref)), out_ref.shape)


def push_kernel(in_ref, price_ref, site_ref, sum_ref, near_ref, far_ref, out_ref, new_ref):
    totals = jnp.sum(in_ref[...].reshape(-1, 8, 128), axis=0)
    new = jnp.clip(site_ref[...] - (price_ref[...] - totals[0:1] / sum_ref[...]), 0.0, 1.0)
    new_ref[...] = new
    push(2.0 * new - site_ref[...], False, tiles(near_ref, far_ref), out_ref)


def spread_kernel(x_ref, marks_ref, out_ref):
    rows = x_ref.shape[0]
    marks = positions(marks_ref[...])
    q, h = kinds(rows)
    key = jnp.where((marks >= 0.0) & (q == 0.0), marks * 2.0 + h, -1.0)
    onehot = (iota((rows, 128), 1).astype(F32) == key).astype(BF16)[:, :32]
    spread = exact_pick(onehot, x_ref[...], ((0,), (0,)))
    for s in range(out_ref.shape[0]):
        out_ref[s] = spread


def dual_kernel(in_ref, row_ref, dual_ref, weight_ref, pixel_ref, new_dual_ref, new_pixel_ref):
    pushed = jnp.sum(in_ref[...], axis=0)
    new_pixel_ref[...], new_dual_ref[...] = step(
        pixel_ref[...], dual_ref[...], weight_ref[...], pushed, row_ref[...]
    )


def local(
    n_pix,
    n_site,
    margins,
    block_pos,
    pattern_ids,
    pattern_gain,
    site_price,
    weights,
    site_start,
    pixel_start,
    dual_start,
):
    slots = margins.shape[0]
    rows = 4 * slots
    chunks = 16
    to_pix = lambda x: lax.all_to_all(x.reshape(n_pix, -1, 128), "pix", 0, 0, tiled=True).reshape(-1, 128)
    to_site = lambda x: lax.all_to_all(x, "site", 0, 0, tiled=True)
    price, site0 = site_price.reshape(1, 128), site_start.reshape(1, 128)
    dual0, weight, pixel0 = (v.reshape(32, 128) for v in (dual_start, weights, pixel_start))

    pairs, near = slots // 2, slots * 9 // 32 // 2 * 2
    far = pairs - near
    (copies,) = call(
        prepare_kernel,
        [((n_pix, 32, 128), BF16)],
        in_hbm(dual0),
        scratch=[pltpu.VMEM((32, 128), F32), pltpu.SemaphoreType.DMA],
        specs=[HBM],
    )
    gathered = to_pix(copies)
    near_tiles, far_tiles, sums, marks, pick = call(
        functools.partial(build_kernel, chunks),
        [
            ((near, 256, 256), BF16),
            pltpu.HBM((far, 256, 256), BF16),
            ((8, 128), F32),
            ((rows, 128), F32),
            ((rows, 32 * n_pix), BF16),
        ],
        *(
            in_hbm(v)
            for v in (margins, block_pos.reshape(1, slots), pattern_ids.reshape(1, 128), pattern_gain)
        ),
        scratch=[
            pltpu.VMEM(margins.shape, jnp.int32),
            pltpu.VMEM((far, 256, 256), BF16),
            pltpu.VMEM((256, 128), F32),
            pltpu.VMEM((1, slots), jnp.int32),
            pltpu.VMEM((1, 128), jnp.int32),
            pltpu.VMEM(pattern_gain.shape, F32),
            pltpu.SemaphoreType.DMA((chunks,)),
            pltpu.SemaphoreType.DMA((3,)),
            pltpu.SemaphoreType.DMA((chunks,)),
        ],
        specs=[HBM] * 4,
        flops=10 * margins.size,
        nbytes=6 * margins.size,
        mib=24,
    )
    message = ((rows, 128), F32)
    out, far_tiles = call(
        first_pull_kernel,
        [message, ((far, 256, 256), BF16)],
        gathered,
        pick,
        marks,
        near_tiles,
        in_hbm(far_tiles),
        sums,
        scratch=[pltpu.VMEM((rows, 128), F32), pltpu.SemaphoreType.DMA],
        specs=[VMEM] * 4 + [HBM, VMEM],
    )
    cov = (near_tiles, far_tiles)
    summed = to_pix(out)
    out, site1, column_sum = call(
        first_push_kernel, [message, ((1, 128), F32), ((1, 128), F32)], summed, price, site0, *cov
    )
    (out,) = call(first_spread_kernel, [((n_site, 64, 128), F32)], to_pix(out), summed)
    out, dual1, pixel1, row_sum = call(
        first_dual_kernel, [message] + [((32, 128), F32)] * 3, to_site(out), summed, dual0, weight, pixel0
    )
    (out,) = call(pull_kernel, [message], to_pix(out), *cov)
    out, site2 = call(push_kernel, [message, ((1, 128), F32)], to_pix(out), price, site1, column_sum, *cov)
    (out,) = call(spread_kernel, [((n_site, 32, 128), F32)], to_pix(out), summed)
    dual2, pixel2 = call(dual_kernel, [((32, 128), F32)] * 2, to_site(out), row_sum, dual1, weight, pixel1)
    return site2.reshape(-1), pixel2.reshape(-1), dual2.reshape(-1)


def solution(mesh):
    placed = (
        P("pix", None, "site"),
        P("pix", "site"),
        P("site"),
        P(),
        P("site"),
        P("pix"),
        P("site"),
        P("pix"),
        P("pix"),
    )
    return jax.shard_map(
        functools.partial(local, mesh.shape["pix"], mesh.shape["site"]),
        mesh=mesh,
        in_specs=placed,
        out_specs=(P("site"), P("pix"), P("pix")),
        check_vma=False,
    )
```

```python
import functools

import jax
import jax.numpy as jnp
from jax import lax
from jax.experimental import pallas as pl
from jax.experimental.pallas import tpu as pltpu
from jax.sharding import PartitionSpec as P

F32 = jnp.float32
BF16 = jnp.bfloat16
HALF_SCALE = 2.0 ** (-10)
VMEM = pl.BlockSpec(memory_space=pltpu.VMEM)
HBM = pl.BlockSpec(memory_space=pltpu.HBM)


def iota(shape, dim):
    return lax.broadcasted_iota(jnp.int32, shape, dim)


def dot(a, b, dims=((1,), (0,))):
    return lax.dot_general(a, b, (dims, ((), ())), preferred_element_type=F32)


def exact_pick(onehot, values, dims):
    high = values.astype(BF16)
    rest = values - high.astype(F32)
    middle = rest.astype(BF16)
    low = (rest - middle.astype(F32)).astype(BF16)
    return dot(onehot, high, dims) + (dot(onehot, middle, dims) + dot(onehot, low, dims))


def call(body, outs, *args, scratch=(), specs=None, flops=0, nbytes=0, mib=8):
    return pl.pallas_call(
        body,
        out_shape=[jax.ShapeDtypeStruct(*o) for o in outs],
        in_specs=specs or [VMEM] * len(args),
        out_specs=[VMEM] * len(outs),
        scratch_shapes=list(scratch),
        cost_estimate=pl.CostEstimate(flops=flops, transcendentals=0, bytes_accessed=nbytes),
        compiler_params=pltpu.CompilerParams(vmem_limit_bytes=mib * 1024 * 1024),
    )(*args)


def in_hbm(value):
    return pltpu.with_memory_space_constraint(value, pltpu.HBM)


def prepare_kernel(dual_hbm, out_ref, dual_ref, sem):
    copy = pltpu.make_async_copy(dual_hbm, dual_ref, sem)
    copy.start()
    copy.wait()
    dual = dual_ref[...].astype(BF16)
    for t in range(out_ref.shape[0]):
        out_ref[t] = dual


AHEAD = 6


def fetch(m_hbm, buf, sems, first, last):
    copies = []
    for c, t in enumerate(range(first, last, 2)):
        part = (m_hbm.at[pl.ds(2 * t, 4)], buf.at[pl.ds(2 * (t - first), 4)])
        copies.append(pltpu.make_async_copy(*part, sems.at[c]))
    for copy in copies[:AHEAD]:
        copy.start()
    return copies


def arrive(copies, c):
    copies[c].wait()
    for copy in copies[c + AHEAD : c + AHEAD + 1]:
        copy.start()


def build(buf, out_ref, half_gain, t):
    def pair(n, carry):
        gain = half_gain[...]
        level = jnp.concatenate([buf[2 * n + i].astype(F32) * HALF_SCALE + gain for i in range(2)], axis=1)
        out_ref[n] = (0.5 * jnp.tanh(level) + 0.5).astype(BF16)
        return carry

    pair(t, 0)
    pair(t + 1, 0)


def build_kernel(
    m_hbm,
    pos_hbm,
    ids_hbm,
    gain_hbm,
    near_ref,
    map_ref,
    note_ref,
    half_gain,
    buf,
    pos_ref,
    ids_ref,
    gain_ref,
    sems,
    small_sems,
):
    small = [(pos_hbm, pos_ref), (ids_hbm, ids_ref), (gain_hbm, gain_ref)]
    small = [pltpu.make_async_copy(src, dst, small_sems.at[n]) for n, (src, dst) in enumerate(small)]
    for copy in small:
        copy.start()
    copies = fetch(m_hbm, buf, sems, 0, near_ref.shape[0])
    for copy in small:
        copy.wait()
    slots = m_hbm.shape[0]
    patterns = gain_ref.shape[0]
    onehot = (ids_ref[...] == iota((patterns, 128), 0)).astype(BF16)
    half_gain[...] = 0.5 * gain_pick(gain_ref[...], onehot)
    wide = jnp.broadcast_to(pos_ref[...].astype(F32), (128, slots)).astype(BF16)
    slot, row = iota((4 * slots, slots), 1), iota((4 * slots, slots), 0)
    map_ref[...] = dot((slot == 2 * (row >> 3) + ((row >> 1) & 1)).astype(BF16), wide, ((1,), (1,)))
    slot, row = iota((2 * slots, slots), 1), iota((2 * slots, slots), 0)
    note_ref[...] = dot((slot == 2 * (row >> 2) + (row & 1)).astype(BF16), wide, ((1,), (1,)))
    for c in range(len(copies)):
        arrive(copies, c)
        build(buf, near_ref, half_gain, 2 * c)


def gain_pick(gain, onehot):
    dims = ((0,), (0,))
    high = gain.astype(BF16)
    rest = gain - high.astype(F32)
    middle = rest.astype(BF16)
    low = (rest - middle.astype(F32)).astype(BF16)
    return dot(high, onehot, dims) + (dot(middle, onehot, dims) + dot(low, onehot, dims))


def tiles(*refs):
    return [ref.at[t] for ref in refs for t in range(ref.shape[0])]


def pull(rows, cov):
    total = 0.0
    for x, tile in zip(rows, cov):
        first = (iota(x.shape, 0) & 1) == 0
        left = jnp.concatenate([jnp.where(first, x, 0.0), jnp.where(first, 0.0, x)], axis=1)
        total = total + dot(left.astype(BF16), tile[...])
    return total


def own_columns(total, kind):
    rows = total[4 * kind : 4 * kind + 4]
    own = jnp.where(iota((4, 128), 0) < 2, rows[:, :128], rows[:, 128:])
    return jnp.sum(own, axis=0, keepdims=True)


def push(row, plain, cov, out_ref):
    spot = iota((8, 128), 0)
    value = jnp.broadcast_to(row, (8, 128))
    if plain:
        value = jnp.where(spot < 4, 1.0, value)
    own = (spot & 2) == 0
    left = jnp.concatenate([jnp.where(own, value, 0.0), jnp.where(own, 0.0, value)], axis=1).astype(BF16)
    first = (spot & 1) == 0
    held = None
    for t, tile in enumerate(cov):
        product = dot(left, tile[...], ((1,), (1,)))
        rows = jnp.where(first, product[:, :128], product[:, 128:])
        if plain:
            out_ref[t * 8 : (t + 1) * 8, :] = rows
        elif t % 2 == 0:
            held = rows
        else:
            out_ref[t * 4 - 4 : t * 4 + 4, :] = jnp.where(spot < 4, held, rows)


def first_pull_kernel(ag_ref, map_ref, note_ref, half_gain, near_ref, m_hbm, out_ref, far_ref, pick_ref, buf, sems):
    rows = map_ref.shape[0]
    near, pairs = near_ref.shape[0], ag_ref.shape[0]
    copies = fetch(m_hbm, buf, sems, near, pairs)
    marks = map_ref[...]
    row = iota((rows, 128), 0)
    key = jnp.where((marks >= 0.0) & ((row & 4) == 0), marks * 2.0 + (row & 1).astype(F32), -1.0)
    pick_ref[...] = (iota((rows, 128), 1).astype(F32) == key).astype(F32)
    plain = iota((8, 128), 0) >= 4

    def message_rows(t):
        part = slice(t * 8, (t + 1) * 8)
        picked = dot(pick_ref[part, :32].astype(BF16), ag_ref[t])
        return jnp.where(plain, (map_ref[part, :] >= 0.0).astype(F32), picked)

    total = pull([message_rows(t) for t in range(near)], tiles(near_ref))
    late = [message_rows(t) for t in range(near, pairs)]
    far = tiles(far_ref)
    for c in range(len(copies)):
        arrive(copies, c)
        build(buf, far_ref, half_gain, 2 * c)
        part = slice(2 * c, 2 * c + 2)
        total = total + pull(late[part], far[part])
    sums, pulled = own_columns(total, 1), own_columns(total, 0)
    place = iota(out_ref.shape, 0) & 3
    out_ref[...] = jnp.where(place == 0, sums, jnp.where(place == 1, pulled, note_ref[...]))


def first_push_kernel(in_ref, price_ref, site_ref, near_ref, far_ref, out_ref, new_ref, sum_ref):
    totals = jnp.sum(in_ref[...].reshape(-1, 8, 128), axis=0)
    column_sum = totals[0:1] + totals[4:5]
    pulled = totals[1:2] + totals[5:6]
    new = jnp.clip(site_ref[...] - (price_ref[...] - pulled / column_sum), 0.0, 1.0)
    new_ref[...] = new
    sum_ref[...] = column_sum
    push(2.0 * new - site_ref[...], True, tiles(near_ref, far_ref), out_ref)


def first_spread_kernel(x_ref, note_ref, out_ref, key_ref):
    notes = note_ref[...].astype(BF16)
    peers = notes.shape[0]

    def positions(rows, shift):
        row, column = iota((rows, peers), 0), iota((rows, peers), 1)
        return dot((column == 4 * (row >> shift) + 2 + ((row >> 1) & 1)).astype(BF16), notes)

    rows = x_ref.shape[0]
    row = iota((rows, 128), 0)
    marks = positions(rows, 3)
    key = jnp.where(marks >= 0.0, ((row >> 2) & 1).astype(F32) * 32.0 + marks * 2.0 + (row & 1).astype(F32), -1.0)
    onehot = (iota((rows, 128), 1).astype(F32) == key).astype(BF16)[:, :64]
    spread = exact_pick(onehot, x_ref[...], ((0,), (0,)))
    for s in range(out_ref.shape[0]):
        out_ref[s] = spread
    row = iota(key_ref.shape, 0)
    marks = positions(key_ref.shape[0], 2)
    key_ref[...] = jnp.where(marks >= 0.0, marks * 2.0 + (row & 1).astype(F32), -1.0)


def chooser(key_ref):
    return (iota(key_ref.shape, 1).astype(F32) == key_ref[...]).astype(BF16)[:, :32]


def step(pixel, dual, weight, pushed, row_sum):
    new = jnp.clip(pixel - (dual - weight), 0.0, 1.0)
    return new, jnp.maximum(dual + ((2.0 * new - pixel) - pushed) / (row_sum + 1.0), 0.0)


def first_dual_kernel(in_ref, key_ref, dual_ref, weight_ref, pixel_ref, out_ref, new_dual_ref, new_pixel_ref, row_ref):
    totals = jnp.sum(in_ref[...], axis=0)
    row_sum = totals[:32]
    row_ref[...] = row_sum
    new_pixel, new_dual = step(pixel_ref[...], dual_ref[...], weight_ref[...], totals[32:], row_sum)
    new_pixel_ref[...] = new_pixel
    new_dual_ref[...] = new_dual
    out_ref[...] = dot(chooser(key_ref), new_dual.astype(BF16))


def pull_kernel(x_ref, near_ref, far_ref, out_ref):
    cov = tiles(near_ref, far_ref)
    total = pull([x_ref[t * 4 : (t + 1) * 4, :] for t in range(len(cov))], cov)
    out_ref[...] = jnp.broadcast_to(own_columns(total, 0), out_ref.shape)


def push_kernel(in_ref, price_ref, site_ref, sum_ref, near_ref, far_ref, out_ref, new_ref):
    pulled = jnp.sum(in_ref[...], axis=0, keepdims=True)
    new = jnp.clip(site_ref[...] - (price_ref[...] - pulled / sum_ref[...]), 0.0, 1.0)
    new_ref[...] = new
    push(2.0 * new - site_ref[...], False, tiles(near_ref, far_ref), out_ref)


def spread_kernel(x_ref, key_ref, out_ref):
    spread = exact_pick(chooser(key_ref), x_ref[...], ((0,), (0,)))
    for s in range(out_ref.shape[0]):
        out_ref[s] = spread


def dual_kernel(in_ref, row_ref, dual_ref, weight_ref, pixel_ref, new_dual_ref, new_pixel_ref):
    pushed = jnp.sum(in_ref[...], axis=0)
    new_pixel_ref[...], new_dual_ref[...] = step(
        pixel_ref[...], dual_ref[...], weight_ref[...], pushed, row_ref[...]
    )


def local(
    n_pix,
    n_site,
    margins,
    block_pos,
    pattern_ids,
    pattern_gain,
    site_price,
    weights,
    site_start,
    pixel_start,
    dual_start,
):
    slots = margins.shape[0]
    rows = 4 * slots
    to_pix = lambda x: lax.all_to_all(x.reshape(n_pix, -1, 128), "pix", 0, 0, tiled=True).reshape(-1, 128)
    to_site = lambda x: lax.all_to_all(x, "site", 0, 0, tiled=True)
    price, site0 = site_price.reshape(1, 128), site_start.reshape(1, 128)
    dual0, weight, pixel0 = (v.reshape(32, 128) for v in (dual_start, weights, pixel_start))

    pairs, near = slots // 2, slots * 11 // 32 // 2 * 2
    far = pairs - near
    (copies,) = call(
        prepare_kernel,
        [((n_pix, 32, 128), BF16)],
        in_hbm(dual0),
        scratch=[pltpu.VMEM((32, 128), F32), pltpu.SemaphoreType.DMA],
        specs=[HBM],
    )
    gathered = to_pix(copies).reshape(n_pix, 32, 128)
    near_tiles, marks, notes, half_gain = call(
        build_kernel,
        [((near, 256, 256), BF16), ((4 * slots, 128), F32), ((2 * slots, 128), F32), ((256, 128), F32)],
        *(in_hbm(v) for v in (margins, block_pos.reshape(1, slots), pattern_ids.reshape(1, 128), pattern_gain)),
        scratch=[
            pltpu.VMEM((2 * near, 256, 128), jnp.int32),
            pltpu.VMEM((1, slots), jnp.int32),
            pltpu.VMEM((1, 128), jnp.int32),
            pltpu.VMEM(pattern_gain.shape, F32),
            pltpu.SemaphoreType.DMA((near // 2,)),
            pltpu.SemaphoreType.DMA((3,)),
        ],
        specs=[HBM] * 4,
        flops=10 * margins.size,
        nbytes=6 * margins.size,
        mib=16,
    )
    message, half_message, line, vector = [((n, 128), F32) for n in (4 * slots, 2 * slots, 1, 32)]
    out, far_tiles = call(
        first_pull_kernel,
        [half_message, ((far, 256, 256), BF16)],
        gathered,
        marks,
        notes,
        half_gain,
        near_tiles,
        in_hbm(margins),
        scratch=[
            pltpu.VMEM((4 * slots, 128), F32),
            pltpu.VMEM((2 * far, 256, 128), jnp.int32),
            pltpu.SemaphoreType.DMA((far // 2,)),
        ],
        specs=[VMEM] * 5 + [HBM],
    )
    cov = (near_tiles, far_tiles)
    summed = to_pix(out)
    out, site1, column_sum = call(first_push_kernel, [message, line, line], summed, price, site0, *cov)
    out, key = call(first_spread_kernel, [((n_site, 64, 128), F32), half_message], to_pix(out), summed)
    out, dual1, pixel1, row_sum = call(
        first_dual_kernel, [half_message] + [vector] * 3, to_site(out), key, dual0, weight, pixel0
    )
    (out,) = call(pull_kernel, [((n_pix, 128), F32)], to_pix(out), *cov)
    out, site2 = call(push_kernel, [half_message, line], to_pix(out), price, site1, column_sum, *cov)
    (out,) = call(spread_kernel, [((n_site, 32, 128), F32)], to_pix(out), key)
    dual2, pixel2 = call(dual_kernel, [vector] * 2, to_site(out), row_sum, dual1, weight, pixel1)
    return site2.reshape(-1), pixel2.reshape(-1), dual2.reshape(-1)


def solution(mesh):
    placed = (
        P("pix", None, "site"),
        P("pix", "site"),
        P("site"),
        P(),
        P("site"),
        P("pix"),
        P("site"),
        P("pix"),
        P("pix"),
    )
    return jax.shard_map(
        functools.partial(local, mesh.shape["pix"], mesh.shape["site"]),
        mesh=mesh,
        in_specs=placed,
        out_specs=(P("site"), P("pix"), P("pix")),
        check_vma=False,
    )
```

```python
import functools

import jax
import jax.numpy as jnp
from jax import lax
from jax.experimental import pallas as pl
from jax.experimental.pallas import tpu as pltpu
from jax.sharding import PartitionSpec as P

F32 = jnp.float32
BF16 = jnp.bfloat16
HALF_SCALE = 2.0 ** (-10)
VMEM = pl.BlockSpec(memory_space=pltpu.VMEM)
HBM = pl.BlockSpec(memory_space=pltpu.HBM)


def iota(shape, dim):
    return lax.broadcasted_iota(jnp.int32, shape, dim)


def dot(a, b, dims=((1,), (0,))):
    return lax.dot_general(a, b, (dims, ((), ())), preferred_element_type=F32)


def exact_pick(onehot, values, dims):
    high = values.astype(BF16)
    rest = values - high.astype(F32)
    middle = rest.astype(BF16)
    low = (rest - middle.astype(F32)).astype(BF16)
    return dot(onehot, high, dims) + (dot(onehot, middle, dims) + dot(onehot, low, dims))


def call(body, outs, *args, scratch=(), specs=None, flops=0, nbytes=0, mib=8):
    return pl.pallas_call(
        body,
        out_shape=[jax.ShapeDtypeStruct(*o) for o in outs],
        in_specs=specs or [VMEM] * len(args),
        out_specs=[VMEM] * len(outs),
        scratch_shapes=list(scratch),
        cost_estimate=pl.CostEstimate(flops=flops, transcendentals=0, bytes_accessed=nbytes),
        compiler_params=pltpu.CompilerParams(vmem_limit_bytes=mib * 1024 * 1024),
    )(*args)


def in_hbm(value):
    return pltpu.with_memory_space_constraint(value, pltpu.HBM)


AHEAD = 6


def fetch(m_hbm, buf, sems, first, last):
    copies = []
    for c, t in enumerate(range(first, last, 2)):
        part = (m_hbm.at[pl.ds(2 * t, 4)], buf.at[pl.ds(2 * (t - first), 4)])
        copies.append(pltpu.make_async_copy(*part, sems.at[c]))
    for copy in copies[:AHEAD]:
        copy.start()
    return copies


def arrive(copies, c):
    copies[c].wait()
    for copy in copies[c + AHEAD : c + AHEAD + 1]:
        copy.start()


def build(buf, out_ref, half_gain, t):
    def pair(n, carry):
        gain = half_gain[...]
        level = jnp.concatenate([buf[2 * n + i].astype(F32) * HALF_SCALE + gain for i in range(2)], axis=1)
        out_ref[n] = (0.5 * jnp.tanh(level) + 0.5).astype(BF16)
        return carry

    pair(t, 0)
    pair(t + 1, 0)


def build_kernel(
    m_hbm,
    pos_hbm,
    ids_hbm,
    gain_hbm,
    near_ref,
    map_ref,
    note_ref,
    half_gain,
    buf,
    pos_ref,
    ids_ref,
    gain_ref,
    sems,
    small_sems,
):
    small = [(pos_hbm, pos_ref), (ids_hbm, ids_ref), (gain_hbm, gain_ref)]
    small = [pltpu.make_async_copy(src, dst, small_sems.at[n]) for n, (src, dst) in enumerate(small)]
    for copy in small:
        copy.start()
    copies = fetch(m_hbm, buf, sems, 0, near_ref.shape[0])
    for copy in small:
        copy.wait()
    slots = m_hbm.shape[0]
    patterns = gain_ref.shape[0]
    onehot = (ids_ref[...] == iota((patterns, 128), 0)).astype(BF16)
    half_gain[...] = 0.5 * gain_pick(gain_ref[...], onehot)
    wide = jnp.broadcast_to(pos_ref[...].astype(F32), (128, slots)).astype(BF16)
    slot, row = iota((4 * slots, slots), 1), iota((4 * slots, slots), 0)
    map_ref[...] = dot((slot == 2 * (row >> 3) + ((row >> 1) & 1)).astype(BF16), wide, ((1,), (1,)))
    slot, row = iota((2 * slots, slots), 1), iota((2 * slots, slots), 0)
    note_ref[...] = dot((slot == 2 * (row >> 2) + (row & 1)).astype(BF16), wide, ((1,), (1,)))
    for c in range(len(copies)):
        arrive(copies, c)
        build(buf, near_ref, half_gain, 2 * c)


def gain_pick(gain, onehot):
    dims = ((0,), (0,))
    high = gain.astype(BF16)
    rest = gain - high.astype(F32)
    middle = rest.astype(BF16)
    low = (rest - middle.astype(F32)).astype(BF16)
    return dot(high, onehot, dims) + (dot(middle, onehot, dims) + dot(low, onehot, dims))


def tiles(*refs):
    return [ref.at[t] for ref in refs for t in range(ref.shape[0])]


def pull(rows, cov):
    total = 0.0
    for x, tile in zip(rows, cov):
        first = (iota(x.shape, 0) & 1) == 0
        left = jnp.concatenate([jnp.where(first, x, 0.0), jnp.where(first, 0.0, x)], axis=1)
        total = total + dot(left.astype(BF16), tile[...])
    return total


def own_columns(total, kind):
    rows = total[4 * kind : 4 * kind + 4]
    own = jnp.where(iota((4, 128), 0) < 2, rows[:, :128], rows[:, 128:])
    return jnp.sum(own, axis=0, keepdims=True)


def push(row, plain, cov, out_ref):
    spot = iota((8, 128), 0)
    value = jnp.broadcast_to(row, (8, 128))
    if plain:
        value = jnp.where(spot < 4, 1.0, value)
    own = (spot & 2) == 0
    left = jnp.concatenate([jnp.where(own, value, 0.0), jnp.where(own, 0.0, value)], axis=1).astype(BF16)
    first = (spot & 1) == 0
    for t, tile in enumerate(cov):
        product = dot(left, tile[...], ((1,), (1,)))
        rows = jnp.where(first, product[:, :128], product[:, 128:])
        if plain:
            out_ref[t * 8 : (t + 1) * 8, :] = rows
        else:
            out_ref[t * 4 : t * 4 + 4, :] = rows[:4]


def first_pull_kernel(ag_ref, map_ref, note_ref, half_gain, near_ref, m_hbm, out_ref, far_ref, pick_ref, buf, sems):
    rows = map_ref.shape[0]
    near, pairs = near_ref.shape[0], ag_ref.shape[0]
    copies = fetch(m_hbm, buf, sems, near, pairs)
    marks = map_ref[...]
    row = iota((rows, 128), 0)
    key = jnp.where((marks >= 0.0) & ((row & 4) == 0), marks * 2.0 + (row & 1).astype(F32), -1.0)
    pick_ref[...] = (iota((rows, 128), 1).astype(F32) == key).astype(F32)
    plain = iota((8, 128), 0) >= 4

    def message_rows(t):
        part = slice(t * 8, (t + 1) * 8)
        picked = dot(pick_ref[part, :32].astype(BF16), ag_ref[t])
        return jnp.where(plain, (map_ref[part, :] >= 0.0).astype(F32), picked)

    total = pull([message_rows(t) for t in range(near)], tiles(near_ref))
    late = [message_rows(t) for t in range(near, pairs)]
    far = tiles(far_ref)
    for c in range(len(copies)):
        arrive(copies, c)
        build(buf, far_ref, half_gain, 2 * c)
        part = slice(2 * c, 2 * c + 2)
        total = total + pull(late[part], far[part])
    sums, pulled = own_columns(total, 1), own_columns(total, 0)
    place = iota(out_ref.shape, 0) & 3
    out_ref[...] = jnp.where(place == 0, sums, jnp.where(place == 1, pulled, note_ref[...]))


def first_push_kernel(in_ref, price_ref, site_ref, near_ref, far_ref, out_ref, new_ref, sum_ref):
    totals = jnp.sum(in_ref[...].reshape(-1, 8, 128), axis=0)
    column_sum = totals[0:1] + totals[4:5]
    pulled = totals[1:2] + totals[5:6]
    new = jnp.clip(site_ref[...] - (price_ref[...] - pulled / column_sum), 0.0, 1.0)
    new_ref[...] = new
    sum_ref[...] = column_sum
    push(2.0 * new - site_ref[...], True, tiles(near_ref, far_ref), out_ref)


def first_spread_kernel(x_ref, note_ref, out_ref, key_ref):
    notes = note_ref[...].astype(BF16)
    peers = notes.shape[0]

    def positions(rows, shift):
        row, column = iota((rows, peers), 0), iota((rows, peers), 1)
        return dot((column == 4 * (row >> shift) + 2 + ((row >> 1) & 1)).astype(BF16), notes)

    rows = x_ref.shape[0]
    row = iota((rows, 128), 0)
    marks = positions(rows, 3)
    key = jnp.where(marks >= 0.0, ((row >> 2) & 1).astype(F32) * 32.0 + marks * 2.0 + (row & 1).astype(F32), -1.0)
    onehot = (iota((rows, 128), 1).astype(F32) == key).astype(BF16)[:, :64]
    spread = exact_pick(onehot, x_ref[...], ((0,), (0,)))
    for s in range(out_ref.shape[0]):
        out_ref[s] = spread
    row = iota(key_ref.shape, 0)
    marks = positions(key_ref.shape[0], 2)
    key_ref[...] = jnp.where(marks >= 0.0, marks * 2.0 + (row & 1).astype(F32), -1.0)


def chooser(key_ref):
    return (iota(key_ref.shape, 1).astype(F32) == key_ref[...]).astype(BF16)[:, :32]


def step(pixel, dual, weight, pushed, row_sum):
    new = jnp.clip(pixel - (dual - weight), 0.0, 1.0)
    return new, jnp.maximum(dual + ((2.0 * new - pixel) - pushed) / (row_sum + 1.0), 0.0)


def first_dual_kernel(in_ref, key_ref, dual_ref, weight_ref, pixel_ref, out_ref, new_dual_ref, new_pixel_ref, row_ref):
    totals = jnp.sum(in_ref[...], axis=0)
    row_sum = totals[:32]
    row_ref[...] = row_sum
    new_pixel, new_dual = step(pixel_ref[...], dual_ref[...], weight_ref[...], totals[32:], row_sum)
    new_pixel_ref[...] = new_pixel
    new_dual_ref[...] = new_dual
    out_ref[...] = dot(chooser(key_ref), new_dual.astype(BF16))


def pull_kernel(x_ref, near_ref, far_ref, out_ref):
    cov = tiles(near_ref, far_ref)
    total = pull([x_ref[t * 4 : (t + 1) * 4, :] for t in range(len(cov))], cov)
    out_ref[...] = jnp.broadcast_to(own_columns(total, 0), out_ref.shape)


def push_kernel(in_ref, price_ref, site_ref, sum_ref, near_ref, far_ref, out_ref, new_ref):
    pulled = jnp.sum(in_ref[...], axis=0, keepdims=True)
    new = jnp.clip(site_ref[...] - (price_ref[...] - pulled / sum_ref[...]), 0.0, 1.0)
    new_ref[...] = new
    push(2.0 * new - site_ref[...], False, tiles(near_ref, far_ref), out_ref)


def spread_kernel(x_ref, key_ref, out_ref):
    spread = exact_pick(chooser(key_ref), x_ref[...], ((0,), (0,)))
    for s in range(out_ref.shape[0]):
        out_ref[s] = spread


def dual_kernel(in_ref, row_ref, dual_ref, weight_ref, pixel_ref, new_dual_ref, new_pixel_ref):
    pushed = jnp.sum(in_ref[...], axis=0)
    new_pixel_ref[...], new_dual_ref[...] = step(
        pixel_ref[...], dual_ref[...], weight_ref[...], pushed, row_ref[...]
    )


def local(
    n_pix,
    n_site,
    margins,
    block_pos,
    pattern_ids,
    pattern_gain,
    site_price,
    weights,
    site_start,
    pixel_start,
    dual_start,
):
    slots = margins.shape[0]
    rows = 4 * slots
    to_pix = lambda x: lax.all_to_all(x.reshape(n_pix, -1, 128), "pix", 0, 0, tiled=True).reshape(-1, 128)
    to_site = lambda x: lax.all_to_all(x, "site", 0, 0, tiled=True)
    price, site0 = site_price.reshape(1, 128), site_start.reshape(1, 128)
    dual0, weight, pixel0 = (v.reshape(32, 128) for v in (dual_start, weights, pixel_start))

    pairs, near = slots // 2, slots * 11 // 32 // 2 * 2
    far = pairs - near
    spot = iota((n_pix, 32, 128), 0) + iota((n_pix, 32, 128), 1) + iota((n_pix, 32, 128), 2)
    copies = jnp.where(spot < n_pix * 4096, dual0[None], 0.0).astype(BF16)
    gathered = to_pix(copies).reshape(n_pix, 32, 128)
    near_tiles, marks, notes, half_gain = call(
        build_kernel,
        [((near, 256, 256), BF16), ((4 * slots, 128), F32), ((2 * slots, 128), F32), ((256, 128), F32)],
        *(in_hbm(v) for v in (margins, block_pos.reshape(1, slots), pattern_ids.reshape(1, 128), pattern_gain)),
        scratch=[
            pltpu.VMEM((2 * near, 256, 128), jnp.int32),
            pltpu.VMEM((1, slots), jnp.int32),
            pltpu.VMEM((1, 128), jnp.int32),
            pltpu.VMEM(pattern_gain.shape, F32),
            pltpu.SemaphoreType.DMA((near // 2,)),
            pltpu.SemaphoreType.DMA((3,)),
        ],
        specs=[HBM] * 4,
        flops=10 * margins.size,
        nbytes=6 * margins.size,
        mib=16,
    )
    message, half_message, line, vector = [((n, 128), F32) for n in (4 * slots, 2 * slots, 1, 32)]
    out, far_tiles = call(
        first_pull_kernel,
        [half_message, ((far, 256, 256), BF16)],
        gathered,
        marks,
        notes,
        half_gain,
        near_tiles,
        in_hbm(margins),
        scratch=[
            pltpu.VMEM((4 * slots, 128), F32),
            pltpu.VMEM((2 * far, 256, 128), jnp.int32),
            pltpu.SemaphoreType.DMA((far // 2,)),
        ],
        specs=[VMEM] * 5 + [HBM],
    )
    cov = (near_tiles, far_tiles)
    summed = to_pix(out)
    out, site1, column_sum = call(first_push_kernel, [message, line, line], summed, price, site0, *cov)
    out, key = call(first_spread_kernel, [((n_site, 64, 128), F32), half_message], to_pix(out), summed)
    out, dual1, pixel1, row_sum = call(
        first_dual_kernel, [half_message] + [vector] * 3, to_site(out), key, dual0, weight, pixel0
    )
    (out,) = call(pull_kernel, [((n_pix, 128), F32)], to_pix(out), *cov)
    out, site2 = call(push_kernel, [half_message, line], to_pix(out), price, site1, column_sum, *cov)
    (out,) = call(spread_kernel, [((n_site, 32, 128), F32)], to_pix(out), key)
    dual2, pixel2 = call(dual_kernel, [vector] * 2, to_site(out), row_sum, dual1, weight, pixel1)
    return site2.reshape(-1), pixel2.reshape(-1), dual2.reshape(-1)


def solution(mesh):
    placed = (
        P("pix", None, "site"),
        P("pix", "site"),
        P("site"),
        P(),
        P("site"),
        P("pix"),
        P("site"),
        P("pix"),
        P("pix"),
    )
    return jax.shard_map(
        functools.partial(local, mesh.shape["pix"], mesh.shape["site"]),
        mesh=mesh,
        in_specs=placed,
        out_specs=(P("site"), P("pix"), P("pix")),
        check_vma=False,
    )
```

```python
import functools

import jax
import jax.numpy as jnp
from jax import lax
from jax.experimental import pallas as pl
from jax.experimental.pallas import tpu as pltpu
from jax.sharding import PartitionSpec as P

F32 = jnp.float32
BF16 = jnp.bfloat16
HALF_SCALE = 2.0 ** (-10)
VMEM = pl.BlockSpec(memory_space=pltpu.VMEM)
HBM = pl.BlockSpec(memory_space=pltpu.HBM)


def iota(shape, dim):
    return lax.broadcasted_iota(jnp.int32, shape, dim)


def dot(a, b, dims=((1,), (0,))):
    return lax.dot_general(a, b, (dims, ((), ())), preferred_element_type=F32)


def exact_pick(onehot, values, dims):
    high = values.astype(BF16)
    rest = values - high.astype(F32)
    middle = rest.astype(BF16)
    low = (rest - middle.astype(F32)).astype(BF16)
    return dot(onehot, high, dims) + (dot(onehot, middle, dims) + dot(onehot, low, dims))


def call(body, outs, *args, scratch=(), specs=None, flops=0, nbytes=0, mib=8):
    return pl.pallas_call(
        body,
        out_shape=[jax.ShapeDtypeStruct(*o) for o in outs],
        in_specs=specs or [VMEM] * len(args),
        out_specs=[VMEM] * len(outs),
        scratch_shapes=list(scratch),
        cost_estimate=pl.CostEstimate(flops=flops, transcendentals=0, bytes_accessed=nbytes),
        compiler_params=pltpu.CompilerParams(vmem_limit_bytes=mib * 1024 * 1024),
    )(*args)


def in_hbm(value):
    return pltpu.with_memory_space_constraint(value, pltpu.HBM)


AHEAD = 6
LEAD = 20
SITE_LEAD = 4


def fetch(m_hbm, buf, sems, first, last):
    copies = []
    pairs = m_hbm.shape[0] // 2
    for c, j in enumerate(range(first, last, 2)):
        part = (m_hbm.at[pl.ds(2 * ((j + LEAD) % pairs), 4)], buf.at[pl.ds(2 * (j - first), 4)])
        copies.append(pltpu.make_async_copy(*part, sems.at[c]))
    for copy in copies[:AHEAD]:
        copy.start()
    return copies


def arrive(copies, c):
    copies[c].wait()
    for copy in copies[c + AHEAD : c + AHEAD + 1]:
        copy.start()


def build(buf, out_ref, half_gain, t):
    def pair(n, carry):
        gain = half_gain[...]
        level = jnp.concatenate([buf[2 * n + i].astype(F32) * HALF_SCALE + gain for i in range(2)], axis=1)
        out_ref[n] = (0.5 * jnp.tanh(level) + 0.5).astype(BF16)
        return carry

    pair(t, 0)
    pair(t + 1, 0)


def build_kernel(
    m_hbm,
    pos_hbm,
    ids_hbm,
    gain_hbm,
    near_ref,
    map_ref,
    note_ref,
    half_gain,
    buf,
    pos_ref,
    ids_ref,
    gain_ref,
    sems,
    small_sems,
):
    small = [(pos_hbm, pos_ref), (ids_hbm, ids_ref), (gain_hbm, gain_ref)]
    small = [pltpu.make_async_copy(src, dst, small_sems.at[n]) for n, (src, dst) in enumerate(small)]
    for copy in small:
        copy.start()
    copies = fetch(m_hbm, buf, sems, 0, near_ref.shape[0])
    for copy in small:
        copy.wait()
    slots = m_hbm.shape[0]
    patterns = gain_ref.shape[0]
    onehot = (ids_ref[...] == iota((patterns, 128), 0)).astype(BF16)
    half_gain[...] = 0.5 * gain_pick(gain_ref[...], onehot)
    wide = jnp.broadcast_to(pos_ref[...].astype(F32), (128, slots)).astype(BF16)

    def peer(j):
        return jnp.where(j + LEAD < slots // 2, j + LEAD, j + LEAD - slots // 2)

    slot, row = iota((4 * slots, slots), 1), iota((4 * slots, slots), 0)
    map_ref[...] = dot((slot == 2 * peer(row >> 3) + ((row >> 1) & 1)).astype(BF16), wide, ((1,), (1,)))
    slot, row = iota((2 * slots, slots), 1), iota((2 * slots, slots), 0)
    note_ref[...] = dot((slot == 2 * peer(row >> 2) + (row & 1)).astype(BF16), wide, ((1,), (1,)))
    for c in range(len(copies)):
        arrive(copies, c)
        build(buf, near_ref, half_gain, 2 * c)


def gain_pick(gain, onehot):
    dims = ((0,), (0,))
    high = gain.astype(BF16)
    rest = gain - high.astype(F32)
    middle = rest.astype(BF16)
    low = (rest - middle.astype(F32)).astype(BF16)
    return dot(high, onehot, dims) + (dot(middle, onehot, dims) + dot(low, onehot, dims))


def tiles(*refs):
    return [ref.at[t] for ref in refs for t in range(ref.shape[0])]


def pull(rows, cov):
    total = 0.0
    for x, tile in zip(rows, cov):
        first = (iota(x.shape, 0) & 1) == 0
        left = jnp.concatenate([jnp.where(first, x, 0.0), jnp.where(first, 0.0, x)], axis=1)
        total = total + dot(left.astype(BF16), tile[...])
    return total


def own_columns(total, kind):
    rows = total[4 * kind : 4 * kind + 4]
    own = jnp.where(iota((4, 128), 0) < 2, rows[:, :128], rows[:, 128:])
    return jnp.sum(own, axis=0, keepdims=True)


def push(row, plain, cov, out_ref):
    spot = iota((8, 128), 0)
    value = jnp.broadcast_to(row, (8, 128))
    if plain:
        value = jnp.where(spot < 4, 1.0, value)
    own = (spot & 2) == 0
    left = jnp.concatenate([jnp.where(own, value, 0.0), jnp.where(own, 0.0, value)], axis=1).astype(BF16)
    first = (spot & 1) == 0
    for t, tile in enumerate(cov):
        product = dot(left, tile[...], ((1,), (1,)))
        rows = jnp.where(first, product[:, :128], product[:, 128:])
        if plain:
            out_ref[t * 8 : (t + 1) * 8, :] = rows
        else:
            out_ref[t * 4 : t * 4 + 4, :] = rows[:4]


def first_pull_kernel(ag_ref, map_ref, note_ref, half_gain, near_ref, m_hbm, out_ref, far_ref, pick_ref, buf, sems):
    rows = map_ref.shape[0]
    near, pairs = near_ref.shape[0], ag_ref.shape[0]
    copies = fetch(m_hbm, buf, sems, near, pairs)
    marks = map_ref[...]
    row = iota((rows, 128), 0)
    key = jnp.where((marks >= 0.0) & ((row & 4) == 0), marks * 2.0 + (row & 1).astype(F32), -1.0)
    pick_ref[...] = (iota((rows, 128), 1).astype(F32) == key).astype(F32)
    plain = iota((8, 128), 0) >= 4

    def message_rows(t):
        part = slice(t * 8, (t + 1) * 8)
        picked = dot(pick_ref[part, :32].astype(BF16), ag_ref[t])
        return jnp.where(plain, (map_ref[part, :] >= 0.0).astype(F32), picked)

    total = pull([message_rows(t) for t in range(near)], tiles(near_ref))
    late = [message_rows(t) for t in range(near, pairs)]
    far = tiles(far_ref)
    for c in range(len(copies)):
        arrive(copies, c)
        build(buf, far_ref, half_gain, 2 * c)
        part = slice(2 * c, 2 * c + 2)
        total = total + pull(late[part], far[part])
    sums, pulled = own_columns(total, 1), own_columns(total, 0)
    place = iota(out_ref.shape, 0) & 3
    out_ref[...] = jnp.where(place == 0, sums, jnp.where(place == 1, pulled, note_ref[...]))


def first_push_kernel(in_ref, price_ref, site_ref, near_ref, far_ref, out_ref, new_ref, sum_ref):
    totals = jnp.sum(in_ref[...].reshape(-1, 8, 128), axis=0)
    column_sum = totals[0:1] + totals[4:5]
    pulled = totals[1:2] + totals[5:6]
    new = jnp.clip(site_ref[...] - (price_ref[...] - pulled / column_sum), 0.0, 1.0)
    new_ref[...] = new
    sum_ref[...] = column_sum
    push(2.0 * new - site_ref[...], True, tiles(near_ref, far_ref), out_ref)


def first_spread_kernel(x_ref, note_ref, out_ref, key_ref):
    notes = note_ref[...].astype(BF16)
    peers = notes.shape[0]

    def positions(rows, shift):
        row, column = iota((rows, peers), 0), iota((rows, peers), 1)
        return dot((column == 4 * (row >> shift) + 2 + ((row >> 1) & 1)).astype(BF16), notes)

    rows = x_ref.shape[0]
    row = iota((rows, 128), 0)
    marks = positions(rows, 3)
    key = jnp.where(marks >= 0.0, ((row >> 2) & 1).astype(F32) * 32.0 + marks * 2.0 + (row & 1).astype(F32), -1.0)
    onehot = (iota((rows, 128), 1).astype(F32) == key).astype(BF16)[:, :64]
    spread = exact_pick(onehot, x_ref[...], ((0,), (0,)))
    for s in range(out_ref.shape[0]):
        out_ref[s] = spread
    row = iota(key_ref.shape, 0)
    marks = positions(key_ref.shape[0], 2)
    key_ref[...] = jnp.where(marks >= 0.0, marks * 2.0 + (row & 1).astype(F32), -1.0)


def chooser(key_ref):
    return (iota(key_ref.shape, 1).astype(F32) == key_ref[...]).astype(BF16)[:, :32]


def step(pixel, dual, weight, pushed, row_sum):
    new = jnp.clip(pixel - (dual - weight), 0.0, 1.0)
    return new, jnp.maximum(dual + ((2.0 * new - pixel) - pushed) / (row_sum + 1.0), 0.0)


def first_dual_kernel(in_ref, key_ref, dual_ref, weight_ref, pixel_ref, out_ref, new_dual_ref, new_pixel_ref, row_ref):
    totals = jnp.sum(in_ref[...], axis=0)
    row_sum = totals[:32]
    row_ref[...] = row_sum
    new_pixel, new_dual = step(pixel_ref[...], dual_ref[...], weight_ref[...], totals[32:], row_sum)
    new_pixel_ref[...] = new_pixel
    new_dual_ref[...] = new_dual
    out_ref[...] = dot(chooser(key_ref), new_dual.astype(BF16))


def pull_kernel(x_ref, near_ref, far_ref, out_ref):
    cov = tiles(near_ref, far_ref)
    total = pull([x_ref[t * 4 : (t + 1) * 4, :] for t in range(len(cov))], cov)
    out_ref[...] = jnp.broadcast_to(own_columns(total, 0), out_ref.shape)


def push_kernel(in_ref, price_ref, site_ref, sum_ref, near_ref, far_ref, out_ref, new_ref):
    pulled = jnp.sum(in_ref[...], axis=0, keepdims=True)
    new = jnp.clip(site_ref[...] - (price_ref[...] - pulled / sum_ref[...]), 0.0, 1.0)
    new_ref[...] = new
    push(2.0 * new - site_ref[...], False, tiles(near_ref, far_ref), out_ref)


def spread_kernel(x_ref, key_ref, out_ref):
    spread = exact_pick(chooser(key_ref), x_ref[...], ((0,), (0,)))
    for s in range(out_ref.shape[0]):
        out_ref[s] = spread


def dual_kernel(in_ref, row_ref, dual_ref, weight_ref, pixel_ref, new_dual_ref, new_pixel_ref):
    pushed = jnp.sum(in_ref[...], axis=0)
    new_pixel_ref[...], new_dual_ref[...] = step(
        pixel_ref[...], dual_ref[...], weight_ref[...], pushed, row_ref[...]
    )


def local(
    n_pix,
    n_site,
    margins,
    block_pos,
    pattern_ids,
    pattern_gain,
    site_price,
    weights,
    site_start,
    pixel_start,
    dual_start,
):
    slots = margins.shape[0]
    rows = 4 * slots
    pix_order = [[(j + LEAD) % n_pix for j in range(n_pix)]]
    site_order = [[(j + SITE_LEAD) % n_site for j in range(n_site)]]

    def to_pix(x):
        x = x.reshape(n_pix, -1, 128)
        return lax.all_to_all(x, "pix", 0, 0, tiled=True, axis_index_groups=pix_order).reshape(-1, 128)

    def to_site(x):
        return lax.all_to_all(x, "site", 0, 0, tiled=True, axis_index_groups=site_order)

    price, site0 = site_price.reshape(1, 128), site_start.reshape(1, 128)
    dual0, weight, pixel0 = (v.reshape(32, 128) for v in (dual_start, weights, pixel_start))

    pairs, near = slots // 2, slots * 11 // 32 // 2 * 2
    far = pairs - near
    spot = iota((n_pix, 32, 128), 0) + iota((n_pix, 32, 128), 1) + iota((n_pix, 32, 128), 2)
    copies = jnp.where(spot < n_pix * 4096, dual0[None], 0.0).astype(BF16)
    gathered = to_pix(copies).reshape(n_pix, 32, 128)
    near_tiles, marks, notes, half_gain = call(
        build_kernel,
        [((near, 256, 256), BF16), ((4 * slots, 128), F32), ((2 * slots, 128), F32), ((256, 128), F32)],
        *(in_hbm(v) for v in (margins, block_pos.reshape(1, slots), pattern_ids.reshape(1, 128), pattern_gain)),
        scratch=[
            pltpu.VMEM((2 * near, 256, 128), jnp.int32),
            pltpu.VMEM((1, slots), jnp.int32),
            pltpu.VMEM((1, 128), jnp.int32),
            pltpu.VMEM(pattern_gain.shape, F32),
            pltpu.SemaphoreType.DMA((near // 2,)),
            pltpu.SemaphoreType.DMA((3,)),
        ],
        specs=[HBM] * 4,
        flops=10 * margins.size,
        nbytes=6 * margins.size,
        mib=16,
    )
    message, half_message, line, vector = [((n, 128), F32) for n in (4 * slots, 2 * slots, 1, 32)]
    out, far_tiles = call(
        first_pull_kernel,
        [half_message, ((far, 256, 256), BF16)],
        gathered,
        marks,
        notes,
        half_gain,
        near_tiles,
        in_hbm(margins),
        scratch=[
            pltpu.VMEM((4 * slots, 128), F32),
            pltpu.VMEM((2 * far, 256, 128), jnp.int32),
            pltpu.SemaphoreType.DMA((far // 2,)),
        ],
        specs=[VMEM] * 5 + [HBM],
    )
    cov = (near_tiles, far_tiles)
    summed = to_pix(out)
    out, site1, column_sum = call(first_push_kernel, [message, line, line], summed, price, site0, *cov)
    out, key = call(first_spread_kernel, [((n_site, 64, 128), F32), half_message], to_pix(out), summed)
    out, dual1, pixel1, row_sum = call(
        first_dual_kernel, [half_message] + [vector] * 3, to_site(out), key, dual0, weight, pixel0
    )
    (out,) = call(pull_kernel, [((n_pix, 128), F32)], to_pix(out), *cov)
    out, site2 = call(push_kernel, [half_message, line], to_pix(out), price, site1, column_sum, *cov)
    (out,) = call(spread_kernel, [((n_site, 32, 128), F32)], to_pix(out), key)
    dual2, pixel2 = call(dual_kernel, [vector] * 2, to_site(out), row_sum, dual1, weight, pixel1)
    return site2.reshape(-1), pixel2.reshape(-1), dual2.reshape(-1)


def solution(mesh):
    placed = (
        P("pix", None, "site"),
        P("pix", "site"),
        P("site"),
        P(),
        P("site"),
        P("pix"),
        P("site"),
        P("pix"),
        P("pix"),
    )
    return jax.shard_map(
        functools.partial(local, mesh.shape["pix"], mesh.shape["site"]),
        mesh=mesh,
        in_specs=placed,
        out_specs=(P("site"), P("pix"), P("pix")),
        check_vma=False,
    )
```

```python
import functools

import jax
import jax.numpy as jnp
from jax import lax
from jax.experimental import pallas as pl
from jax.experimental.pallas import tpu as pltpu
from jax.sharding import PartitionSpec as P

F32 = jnp.float32
BF16 = jnp.bfloat16
HALF_SCALE = 2.0 ** (-10)
VMEM = pl.BlockSpec(memory_space=pltpu.VMEM)
HBM = pl.BlockSpec(memory_space=pltpu.HBM)


def iota(shape, dim):
    return lax.broadcasted_iota(jnp.int32, shape, dim)


def dot(a, b, dims=((1,), (0,))):
    return lax.dot_general(a, b, (dims, ((), ())), preferred_element_type=F32)


def exact_pick(onehot, values, dims):
    high = values.astype(BF16)
    rest = values - high.astype(F32)
    middle = rest.astype(BF16)
    low = (rest - middle.astype(F32)).astype(BF16)
    return dot(onehot, high, dims) + (dot(onehot, middle, dims) + dot(onehot, low, dims))


def call(body, outs, *args, scratch=(), specs=None, flops=0, nbytes=0, mib=8):
    return pl.pallas_call(
        body,
        out_shape=[jax.ShapeDtypeStruct(*o) for o in outs],
        in_specs=specs or [VMEM] * len(args),
        out_specs=[VMEM] * len(outs),
        scratch_shapes=list(scratch),
        cost_estimate=pl.CostEstimate(flops=flops, transcendentals=0, bytes_accessed=nbytes),
        compiler_params=pltpu.CompilerParams(vmem_limit_bytes=mib * 1024 * 1024),
    )(*args)


def in_hbm(value):
    return pltpu.with_memory_space_constraint(value, pltpu.HBM)


AHEAD = 6
SITE_ORDER = (4, 6, 0, 2, 5, 7, 1, 3)


def peer(j):
    chip = ((j >> 1) + 10) & 15
    y, x = chip >> 2, chip & 3
    return 8 * y + 2 * (x ^ (3 * (y & 1))) + (j & 1)


def fetch(m_hbm, buf, sems, first, last):
    copies = []
    for c, j in enumerate(range(first, last, 2)):
        part = (m_hbm.at[pl.ds(2 * peer(j), 4)], buf.at[pl.ds(2 * (j - first), 4)])
        copies.append(pltpu.make_async_copy(*part, sems.at[c]))
    for copy in copies[:AHEAD]:
        copy.start()
    return copies


def arrive(copies, c):
    copies[c].wait()
    for copy in copies[c + AHEAD : c + AHEAD + 1]:
        copy.start()


def build(buf, out_ref, half_gain, t):
    def pair(n, carry):
        gain = half_gain[...]
        level = jnp.concatenate([buf[2 * n + i].astype(F32) * HALF_SCALE + gain for i in range(2)], axis=1)
        out_ref[n] = (0.5 * jnp.tanh(level) + 0.5).astype(BF16)
        return carry

    pair(t, 0)
    pair(t + 1, 0)


def build_kernel(
    m_hbm,
    pos_hbm,
    ids_hbm,
    gain_hbm,
    near_ref,
    map_ref,
    note_ref,
    half_gain,
    buf,
    pos_ref,
    ids_ref,
    gain_ref,
    sems,
    small_sems,
):
    small = [(pos_hbm, pos_ref), (ids_hbm, ids_ref), (gain_hbm, gain_ref)]
    small = [pltpu.make_async_copy(src, dst, small_sems.at[n]) for n, (src, dst) in enumerate(small)]
    for copy in small:
        copy.start()
    copies = fetch(m_hbm, buf, sems, 0, near_ref.shape[0])
    for copy in small:
        copy.wait()
    slots = m_hbm.shape[0]
    patterns = gain_ref.shape[0]
    onehot = (ids_ref[...] == iota((patterns, 128), 0)).astype(BF16)
    half_gain[...] = 0.5 * gain_pick(gain_ref[...], onehot)
    wide = jnp.broadcast_to(pos_ref[...].astype(F32), (128, slots)).astype(BF16)
    slot, row = iota((4 * slots, slots), 1), iota((4 * slots, slots), 0)
    map_ref[...] = dot((slot == 2 * peer(row >> 3) + ((row >> 1) & 1)).astype(BF16), wide, ((1,), (1,)))
    slot, row = iota((2 * slots, slots), 1), iota((2 * slots, slots), 0)
    note_ref[...] = dot((slot == 2 * peer(row >> 2) + (row & 1)).astype(BF16), wide, ((1,), (1,)))
    for c in range(len(copies)):
        arrive(copies, c)
        build(buf, near_ref, half_gain, 2 * c)


def gain_pick(gain, onehot):
    dims = ((0,), (0,))
    high = gain.astype(BF16)
    rest = gain - high.astype(F32)
    middle = rest.astype(BF16)
    low = (rest - middle.astype(F32)).astype(BF16)
    return dot(high, onehot, dims) + (dot(middle, onehot, dims) + dot(low, onehot, dims))


def tiles(*refs):
    return [ref.at[t] for ref in refs for t in range(ref.shape[0])]


def pull(rows, cov):
    total = 0.0
    for x, tile in zip(rows, cov):
        first = (iota(x.shape, 0) & 1) == 0
        left = jnp.concatenate([jnp.where(first, x, 0.0), jnp.where(first, 0.0, x)], axis=1)
        total = total + dot(left.astype(BF16), tile[...])
    return total


def own_columns(total, kind):
    rows = total[4 * kind : 4 * kind + 4]
    own = jnp.where(iota((4, 128), 0) < 2, rows[:, :128], rows[:, 128:])
    return jnp.sum(own, axis=0, keepdims=True)


def push(row, plain, cov, out_ref):
    spot = iota((8, 128), 0)
    value = jnp.broadcast_to(row, (8, 128))
    if plain:
        value = jnp.where(spot < 4, 1.0, value)
    own = (spot & 2) == 0
    left = jnp.concatenate([jnp.where(own, value, 0.0), jnp.where(own, 0.0, value)], axis=1).astype(BF16)
    first = (spot & 1) == 0
    for t, tile in enumerate(cov):
        product = dot(left, tile[...], ((1,), (1,)))
        rows = jnp.where(first, product[:, :128], product[:, 128:])
        if plain:
            out_ref[t * 8 : (t + 1) * 8, :] = rows
        else:
            out_ref[t * 4 : t * 4 + 4, :] = rows[:4]


def first_pull_kernel(ag_ref, map_ref, note_ref, half_gain, near_ref, m_hbm, out_ref, far_ref, pick_ref, buf, sems):
    rows = map_ref.shape[0]
    near, pairs = near_ref.shape[0], ag_ref.shape[0]
    copies = fetch(m_hbm, buf, sems, near, pairs)
    marks = map_ref[...]
    row = iota((rows, 128), 0)
    key = jnp.where((marks >= 0.0) & ((row & 4) == 0), marks * 2.0 + (row & 1).astype(F32), -1.0)
    pick_ref[...] = (iota((rows, 128), 1).astype(F32) == key).astype(F32)
    plain = iota((8, 128), 0) >= 4

    def message_rows(t):
        part = slice(t * 8, (t + 1) * 8)
        picked = dot(pick_ref[part, :32].astype(BF16), ag_ref[t])
        return jnp.where(plain, (map_ref[part, :] >= 0.0).astype(F32), picked)

    total = pull([message_rows(t) for t in range(near)], tiles(near_ref))
    late = [message_rows(t) for t in range(near, pairs)]
    far = tiles(far_ref)
    for c in range(len(copies)):
        arrive(copies, c)
        build(buf, far_ref, half_gain, 2 * c)
        part = slice(2 * c, 2 * c + 2)
        total = total + pull(late[part], far[part])
    sums, pulled = own_columns(total, 1), own_columns(total, 0)
    place = iota(out_ref.shape, 0) & 3
    out_ref[...] = jnp.where(place == 0, sums, jnp.where(place == 1, pulled, note_ref[...]))


def first_push_kernel(in_ref, price_ref, site_ref, near_ref, far_ref, out_ref, new_ref, sum_ref):
    totals = jnp.sum(in_ref[...].reshape(-1, 8, 128), axis=0)
    column_sum = totals[0:1] + totals[4:5]
    pulled = totals[1:2] + totals[5:6]
    new = jnp.clip(site_ref[...] - (price_ref[...] - pulled / column_sum), 0.0, 1.0)
    new_ref[...] = new
    sum_ref[...] = column_sum
    push(2.0 * new - site_ref[...], True, tiles(near_ref, far_ref), out_ref)


def first_spread_kernel(x_ref, note_ref, out_ref, key_ref):
    notes = note_ref[...].astype(BF16)
    peers = notes.shape[0]

    def positions(rows, shift):
        row, column = iota((rows, peers), 0), iota((rows, peers), 1)
        return dot((column == 4 * (row >> shift) + 2 + ((row >> 1) & 1)).astype(BF16), notes)

    rows = x_ref.shape[0]
    row = iota((rows, 128), 0)
    marks = positions(rows, 3)
    key = jnp.where(marks >= 0.0, ((row >> 2) & 1).astype(F32) * 32.0 + marks * 2.0 + (row & 1).astype(F32), -1.0)
    onehot = (iota((rows, 128), 1).astype(F32) == key).astype(BF16)[:, :64]
    spread = exact_pick(onehot, x_ref[...], ((0,), (0,)))
    for s in range(out_ref.shape[0]):
        out_ref[s] = spread
    row = iota(key_ref.shape, 0)
    marks = positions(key_ref.shape[0], 2)
    key_ref[...] = jnp.where(marks >= 0.0, marks * 2.0 + (row & 1).astype(F32), -1.0)


def chooser(key_ref):
    return (iota(key_ref.shape, 1).astype(F32) == key_ref[...]).astype(BF16)[:, :32]


def step(pixel, dual, weight, pushed, row_sum):
    new = jnp.clip(pixel - (dual - weight), 0.0, 1.0)
    return new, jnp.maximum(dual + ((2.0 * new - pixel) - pushed) / (row_sum + 1.0), 0.0)


def first_dual_kernel(in_ref, key_ref, dual_ref, weight_ref, pixel_ref, out_ref, new_dual_ref, new_pixel_ref, row_ref):
    totals = jnp.sum(in_ref[...], axis=0)
    row_sum = totals[:32]
    row_ref[...] = row_sum
    new_pixel, new_dual = step(pixel_ref[...], dual_ref[...], weight_ref[...], totals[32:], row_sum)
    new_pixel_ref[...] = new_pixel
    new_dual_ref[...] = new_dual
    out_ref[...] = dot(chooser(key_ref), new_dual.astype(BF16))


def pull_kernel(x_ref, near_ref, far_ref, out_ref):
    cov = tiles(near_ref, far_ref)
    total = pull([x_ref[t * 4 : (t + 1) * 4, :] for t in range(len(cov))], cov)
    out_ref[...] = jnp.broadcast_to(own_columns(total, 0), out_ref.shape)


def push_kernel(in_ref, price_ref, site_ref, sum_ref, near_ref, far_ref, out_ref, new_ref):
    pulled = jnp.sum(in_ref[...], axis=0, keepdims=True)
    new = jnp.clip(site_ref[...] - (price_ref[...] - pulled / sum_ref[...]), 0.0, 1.0)
    new_ref[...] = new
    push(2.0 * new - site_ref[...], False, tiles(near_ref, far_ref), out_ref)


def spread_kernel(x_ref, key_ref, out_ref):
    spread = exact_pick(chooser(key_ref), x_ref[...], ((0,), (0,)))
    for s in range(out_ref.shape[0]):
        out_ref[s] = spread


def dual_kernel(in_ref, row_ref, dual_ref, weight_ref, pixel_ref, new_dual_ref, new_pixel_ref):
    pushed = jnp.sum(in_ref[...], axis=0)
    new_pixel_ref[...], new_dual_ref[...] = step(
        pixel_ref[...], dual_ref[...], weight_ref[...], pushed, row_ref[...]
    )


def local(
    n_pix,
    n_site,
    margins,
    block_pos,
    pattern_ids,
    pattern_gain,
    site_price,
    weights,
    site_start,
    pixel_start,
    dual_start,
):
    slots = margins.shape[0]
    rows = 4 * slots
    pix_order = [[peer(j) for j in range(n_pix)]]

    def to_pix(x):
        x = x.reshape(n_pix, -1, 128)
        return lax.all_to_all(x, "pix", 0, 0, tiled=True, axis_index_groups=pix_order).reshape(-1, 128)

    def to_site(x):
        return lax.all_to_all(x, "site", 0, 0, tiled=True, axis_index_groups=[SITE_ORDER])

    price, site0 = site_price.reshape(1, 128), site_start.reshape(1, 128)
    dual0, weight, pixel0 = (v.reshape(32, 128) for v in (dual_start, weights, pixel_start))

    pairs, near = slots // 2, slots * 11 // 32 // 2 * 2
    far = pairs - near
    spot = iota((n_pix, 32, 128), 0) + iota((n_pix, 32, 128), 1) + iota((n_pix, 32, 128), 2)
    copies = jnp.where(spot < n_pix * 4096, dual0[None], 0.0).astype(BF16)
    gathered = to_pix(copies).reshape(n_pix, 32, 128)
    near_tiles, marks, notes, half_gain = call(
        build_kernel,
        [((near, 256, 256), BF16), ((4 * slots, 128), F32), ((2 * slots, 128), F32), ((256, 128), F32)],
        *(in_hbm(v) for v in (margins, block_pos.reshape(1, slots), pattern_ids.reshape(1, 128), pattern_gain)),
        scratch=[
            pltpu.VMEM((2 * near, 256, 128), jnp.int32),
            pltpu.VMEM((1, slots), jnp.int32),
            pltpu.VMEM((1, 128), jnp.int32),
            pltpu.VMEM(pattern_gain.shape, F32),
            pltpu.SemaphoreType.DMA((near // 2,)),
            pltpu.SemaphoreType.DMA((3,)),
        ],
        specs=[HBM] * 4,
        flops=10 * margins.size,
        nbytes=6 * margins.size,
        mib=16,
    )
    message, half_message, line, vector = [((n, 128), F32) for n in (4 * slots, 2 * slots, 1, 32)]
    out, far_tiles = call(
        first_pull_kernel,
        [half_message, ((far, 256, 256), BF16)],
        gathered,
        marks,
        notes,
        half_gain,
        near_tiles,
        in_hbm(margins),
        scratch=[
            pltpu.VMEM((4 * slots, 128), F32),
            pltpu.VMEM((2 * far, 256, 128), jnp.int32),
            pltpu.SemaphoreType.DMA((far // 2,)),
        ],
        specs=[VMEM] * 5 + [HBM],
    )
    cov = (near_tiles, far_tiles)
    summed = to_pix(out)
    out, site1, column_sum = call(first_push_kernel, [message, line, line], summed, price, site0, *cov)
    out, key = call(first_spread_kernel, [((n_site, 64, 128), F32), half_message], to_pix(out), summed)
    out, dual1, pixel1, row_sum = call(
        first_dual_kernel, [half_message] + [vector] * 3, to_site(out), key, dual0, weight, pixel0
    )
    (out,) = call(pull_kernel, [((n_pix, 128), F32)], to_pix(out), *cov)
    out, site2 = call(push_kernel, [half_message, line], to_pix(out), price, site1, column_sum, *cov)
    (out,) = call(spread_kernel, [((n_site, 32, 128), F32)], to_pix(out), key)
    dual2, pixel2 = call(dual_kernel, [vector] * 2, to_site(out), row_sum, dual1, weight, pixel1)
    return site2.reshape(-1), pixel2.reshape(-1), dual2.reshape(-1)


def solution(mesh):
    placed = (
        P("pix", None, "site"),
        P("pix", "site"),
        P("site"),
        P(),
        P("site"),
        P("pix"),
        P("site"),
        P("pix"),
        P("pix"),
    )
    return jax.shard_map(
        functools.partial(local, mesh.shape["pix"], mesh.shape["site"]),
        mesh=mesh,
        in_specs=placed,
        out_specs=(P("site"), P("pix"), P("pix")),
        check_vma=False,
    )
```

```python
import functools

import jax
import jax.numpy as jnp
from jax import lax
from jax.experimental import pallas as pl
from jax.experimental.pallas import tpu as pltpu
from jax.sharding import PartitionSpec as P

F32 = jnp.float32
BF16 = jnp.bfloat16
HALF_SCALE = 2.0 ** (-10)
VMEM = pl.BlockSpec(memory_space=pltpu.VMEM)
HBM = pl.BlockSpec(memory_space=pltpu.HBM)


def iota(shape, dim):
    return lax.broadcasted_iota(jnp.int32, shape, dim)


def dot(a, b, dims=((1,), (0,))):
    return lax.dot_general(a, b, (dims, ((), ())), preferred_element_type=F32)


def exact_pick(onehot, values, dims):
    high = values.astype(BF16)
    rest = values - high.astype(F32)
    middle = rest.astype(BF16)
    low = (rest - middle.astype(F32)).astype(BF16)
    return dot(onehot, high, dims) + (dot(onehot, middle, dims) + dot(onehot, low, dims))


def call(body, outs, *args, scratch=(), specs=None, flops=0, nbytes=0, mib=8):
    return pl.pallas_call(
        body,
        out_shape=[jax.ShapeDtypeStruct(*o) for o in outs],
        in_specs=specs or [VMEM] * len(args),
        out_specs=[VMEM] * len(outs),
        scratch_shapes=list(scratch),
        cost_estimate=pl.CostEstimate(flops=flops, transcendentals=0, bytes_accessed=nbytes),
        compiler_params=pltpu.CompilerParams(vmem_limit_bytes=mib * 1024 * 1024),
    )(*args)


def in_hbm(value):
    return pltpu.with_memory_space_constraint(value, pltpu.HBM)


AHEAD = 6
SITE_ORDER = (4, 0, 2, 7, 1, 6, 3, 5)


def peer(j):
    chip = ((j >> 1) + 10) & 15
    y, x = chip >> 2, chip & 3
    return 8 * y + 2 * (x ^ (3 * (y & 1))) + (j & 1)


def fetch(m_hbm, buf, sems, first, last):
    copies = []
    for c, j in enumerate(range(first, last, 2)):
        part = (m_hbm.at[pl.ds(2 * peer(j), 4)], buf.at[pl.ds(2 * (j - first), 4)])
        copies.append(pltpu.make_async_copy(*part, sems.at[c]))
    for copy in copies[:AHEAD]:
        copy.start()
    return copies


def arrive(copies, c):
    copies[c].wait()
    for copy in copies[c + AHEAD : c + AHEAD + 1]:
        copy.start()


def build(buf, out_ref, half_gain, t):
    def pair(n, carry):
        gain = half_gain[...]
        level = jnp.concatenate([buf[2 * n + i].astype(F32) * HALF_SCALE + gain for i in range(2)], axis=1)
        out_ref[n] = (jnp.tanh(level) + 1.0).astype(BF16)
        return carry

    pair(t, 0)
    pair(t + 1, 0)


def build_kernel(
    m_hbm,
    pos_hbm,
    ids_hbm,
    gain_hbm,
    near_ref,
    map_ref,
    note_ref,
    half_gain,
    buf,
    pos_ref,
    ids_ref,
    gain_ref,
    sems,
    small_sems,
):
    small = [(pos_hbm, pos_ref), (ids_hbm, ids_ref), (gain_hbm, gain_ref)]
    small = [pltpu.make_async_copy(src, dst, small_sems.at[n]) for n, (src, dst) in enumerate(small)]
    for copy in small:
        copy.start()
    copies = fetch(m_hbm, buf, sems, 0, near_ref.shape[0])
    for copy in small:
        copy.wait()
    slots = m_hbm.shape[0]
    patterns = gain_ref.shape[0]
    onehot = (ids_ref[...] == iota((patterns, 128), 0)).astype(BF16)
    half_gain[...] = 0.5 * gain_pick(gain_ref[...], onehot)
    wide = jnp.broadcast_to(pos_ref[...].astype(F32), (128, slots)).astype(BF16)
    slot, row = iota((4 * slots, slots), 1), iota((4 * slots, slots), 0)
    map_ref[...] = dot((slot == 2 * peer(row >> 3) + ((row >> 1) & 1)).astype(BF16), wide, ((1,), (1,)))
    slot, row = iota((2 * slots, slots), 1), iota((2 * slots, slots), 0)
    note_ref[...] = dot((slot == 2 * peer(row >> 2) + (row & 1)).astype(BF16), wide, ((1,), (1,)))
    for c in range(len(copies)):
        arrive(copies, c)
        build(buf, near_ref, half_gain, 2 * c)


def gain_pick(gain, onehot):
    dims = ((0,), (0,))
    high = gain.astype(BF16)
    rest = gain - high.astype(F32)
    middle = rest.astype(BF16)
    low = (rest - middle.astype(F32)).astype(BF16)
    return dot(high, onehot, dims) + (dot(middle, onehot, dims) + dot(low, onehot, dims))


def tiles(*refs):
    return [ref.at[t] for ref in refs for t in range(ref.shape[0])]


def pull(rows, cov):
    total = 0.0
    for x, tile in zip(rows, cov):
        first = (iota(x.shape, 0) & 1) == 0
        left = jnp.concatenate([jnp.where(first, x, 0.0), jnp.where(first, 0.0, x)], axis=1)
        total = total + dot(left.astype(BF16), tile[...])
    return total


def own_columns(total, kind):
    rows = total[4 * kind : 4 * kind + 4]
    own = jnp.where(iota((4, 128), 0) < 2, rows[:, :128], rows[:, 128:])
    return jnp.sum(own, axis=0, keepdims=True)


def push(row, plain, cov, out_ref):
    spot = iota((8, 128), 0)
    value = jnp.broadcast_to(0.5 * row, (8, 128))
    if plain:
        value = jnp.where(spot < 4, 0.5, value)
    own = (spot & 2) == 0
    left = jnp.concatenate([jnp.where(own, value, 0.0), jnp.where(own, 0.0, value)], axis=1).astype(BF16)
    first = (spot & 1) == 0
    for t, tile in enumerate(cov):
        product = dot(left, tile[...], ((1,), (1,)))
        rows = jnp.where(first, product[:, :128], product[:, 128:])
        if plain:
            out_ref[t * 8 : (t + 1) * 8, :] = rows
        else:
            out_ref[t * 4 : t * 4 + 4, :] = rows[:4]


def first_pull_kernel(ag_ref, map_ref, note_ref, half_gain, near_ref, m_hbm, out_ref, far_ref, pick_ref, buf, sems):
    rows = map_ref.shape[0]
    near, pairs = near_ref.shape[0], ag_ref.shape[0]
    copies = fetch(m_hbm, buf, sems, near, pairs)
    marks = map_ref[...]
    row = iota((rows, 128), 0)
    key = jnp.where((marks >= 0.0) & ((row & 4) == 0), marks * 2.0 + (row & 1).astype(F32), -1.0)
    pick_ref[...] = (iota((rows, 128), 1).astype(F32) == key).astype(F32)
    plain = iota((8, 128), 0) >= 4

    def message_rows(t):
        part = slice(t * 8, (t + 1) * 8)
        picked = dot(pick_ref[part, :32].astype(BF16), ag_ref[t])
        return jnp.where(plain, (map_ref[part, :] >= 0.0).astype(F32), picked)

    total = pull([message_rows(t) for t in range(near)], tiles(near_ref))
    late = [message_rows(t) for t in range(near, pairs)]
    far = tiles(far_ref)
    for c in range(len(copies)):
        arrive(copies, c)
        build(buf, far_ref, half_gain, 2 * c)
        part = slice(2 * c, 2 * c + 2)
        total = total + pull(late[part], far[part])
    sums, pulled = own_columns(total, 1), own_columns(total, 0)
    place = iota(out_ref.shape, 0) & 3
    out_ref[...] = jnp.where(place == 0, sums, jnp.where(place == 1, pulled, note_ref[...]))


def first_push_kernel(in_ref, price_ref, site_ref, near_ref, far_ref, out_ref, new_ref, sum_ref):
    totals = jnp.sum(in_ref[...].reshape(-1, 8, 128), axis=0)
    column_sum = totals[0:1] + totals[4:5]
    pulled = totals[1:2] + totals[5:6]
    new = jnp.clip(site_ref[...] - (price_ref[...] - pulled / column_sum), 0.0, 1.0)
    new_ref[...] = new
    sum_ref[...] = column_sum
    push(2.0 * new - site_ref[...], True, tiles(near_ref, far_ref), out_ref)


def first_spread_kernel(x_ref, note_ref, out_ref, key_ref):
    notes = note_ref[...].astype(BF16)
    peers = notes.shape[0]

    def positions(rows, shift):
        row, column = iota((rows, peers), 0), iota((rows, peers), 1)
        return dot((column == 4 * (row >> shift) + 2 + ((row >> 1) & 1)).astype(BF16), notes)

    rows = x_ref.shape[0]
    row = iota((rows, 128), 0)
    marks = positions(rows, 3)
    key = jnp.where(marks >= 0.0, ((row >> 2) & 1).astype(F32) * 32.0 + marks * 2.0 + (row & 1).astype(F32), -1.0)
    onehot = (iota((rows, 128), 1).astype(F32) == key).astype(BF16)[:, :64]
    spread = exact_pick(onehot, x_ref[...], ((0,), (0,)))
    for s in range(out_ref.shape[0]):
        out_ref[s] = spread
    row = iota(key_ref.shape, 0)
    marks = positions(key_ref.shape[0], 2)
    key_ref[...] = jnp.where(marks >= 0.0, marks * 2.0 + (row & 1).astype(F32), -1.0)


def chooser(key_ref):
    return (iota(key_ref.shape, 1).astype(F32) == key_ref[...]).astype(BF16)[:, :32]


def step(pixel, dual, weight, pushed, row_sum):
    new = jnp.clip(pixel - (dual - weight), 0.0, 1.0)
    return new, jnp.maximum(dual + ((2.0 * new - pixel) - pushed) / (row_sum + 1.0), 0.0)


def first_dual_kernel(in_ref, key_ref, dual_ref, weight_ref, pixel_ref, out_ref, new_dual_ref, new_pixel_ref, row_ref):
    totals = jnp.sum(in_ref[...], axis=0)
    row_sum = totals[:32]
    row_ref[...] = row_sum
    new_pixel, new_dual = step(pixel_ref[...], dual_ref[...], weight_ref[...], totals[32:], row_sum)
    new_pixel_ref[...] = new_pixel
    new_dual_ref[...] = new_dual
    out_ref[...] = dot(chooser(key_ref), new_dual.astype(BF16)).astype(BF16)


def pull_kernel(x_ref, near_ref, far_ref, out_ref, rows_ref):
    cov = tiles(near_ref, far_ref)
    rows_ref[...] = x_ref[...].astype(F32)
    total = pull([rows_ref[t * 4 : (t + 1) * 4, :] for t in range(len(cov))], cov)
    out_ref[...] = jnp.broadcast_to(own_columns(total, 0), out_ref.shape)


def push_kernel(in_ref, price_ref, site_ref, sum_ref, near_ref, far_ref, out_ref, new_ref):
    pulled = jnp.sum(in_ref[...], axis=0, keepdims=True)
    new = jnp.clip(site_ref[...] - (price_ref[...] - pulled / sum_ref[...]), 0.0, 1.0)
    new_ref[...] = new
    push(2.0 * new - site_ref[...], False, tiles(near_ref, far_ref), out_ref)


def spread_kernel(x_ref, key_ref, out_ref):
    spread = exact_pick(chooser(key_ref), x_ref[...], ((0,), (0,)))
    for s in range(out_ref.shape[0]):
        out_ref[s] = spread


def dual_kernel(in_ref, row_ref, dual_ref, weight_ref, pixel_ref, new_dual_ref, new_pixel_ref):
    pushed = jnp.sum(in_ref[...], axis=0)
    new_pixel_ref[...], new_dual_ref[...] = step(
        pixel_ref[...], dual_ref[...], weight_ref[...], pushed, row_ref[...]
    )


def local(
    n_pix,
    n_site,
    margins,
    block_pos,
    pattern_ids,
    pattern_gain,
    site_price,
    weights,
    site_start,
    pixel_start,
    dual_start,
):
    slots = margins.shape[0]
    rows = 4 * slots
    pix_order = [[peer(j) for j in range(n_pix)]]

    def to_pix(x):
        x = x.reshape(n_pix, -1, 128)
        return lax.all_to_all(x, "pix", 0, 0, tiled=True, axis_index_groups=pix_order).reshape(-1, 128)

    def to_site(x):
        return lax.all_to_all(x, "site", 0, 0, tiled=True, axis_index_groups=[SITE_ORDER])

    price, site0 = site_price.reshape(1, 128), site_start.reshape(1, 128)
    dual0, weight, pixel0 = (v.reshape(32, 128) for v in (dual_start, weights, pixel_start))

    pairs, near = slots // 2, slots * 11 // 32 // 2 * 2
    far = pairs - near
    spot = iota((n_pix, 32, 128), 0) + iota((n_pix, 32, 128), 1) + iota((n_pix, 32, 128), 2)
    copies = jnp.where(spot < n_pix * 4096, dual0[None], 0.0).astype(BF16)
    gathered = to_pix(copies).reshape(n_pix, 32, 128)
    near_tiles, marks, notes, half_gain = call(
        build_kernel,
        [((near, 256, 256), BF16), ((4 * slots, 128), F32), ((2 * slots, 128), F32), ((256, 128), F32)],
        *(in_hbm(v) for v in (margins, block_pos.reshape(1, slots), pattern_ids.reshape(1, 128), pattern_gain)),
        scratch=[
            pltpu.VMEM((2 * near, 256, 128), jnp.int32),
            pltpu.VMEM((1, slots), jnp.int32),
            pltpu.VMEM((1, 128), jnp.int32),
            pltpu.VMEM(pattern_gain.shape, F32),
            pltpu.SemaphoreType.DMA((near // 2,)),
            pltpu.SemaphoreType.DMA((3,)),
        ],
        specs=[HBM] * 4,
        flops=10 * margins.size,
        nbytes=6 * margins.size,
        mib=16,
    )
    message, half_message, line, vector = [((n, 128), F32) for n in (4 * slots, 2 * slots, 1, 32)]
    out, far_tiles = call(
        first_pull_kernel,
        [half_message, ((far, 256, 256), BF16)],
        gathered,
        marks,
        notes,
        half_gain,
        near_tiles,
        in_hbm(margins),
        scratch=[
            pltpu.VMEM((4 * slots, 128), F32),
            pltpu.VMEM((2 * far, 256, 128), jnp.int32),
            pltpu.SemaphoreType.DMA((far // 2,)),
        ],
        specs=[VMEM] * 5 + [HBM],
    )
    cov = (near_tiles, far_tiles)
    summed = to_pix(out)
    out, site1, column_sum = call(first_push_kernel, [message, line, line], summed, price, site0, *cov)
    out, key = call(first_spread_kernel, [((n_site, 64, 128), F32), half_message], to_pix(out), summed)
    out, dual1, pixel1, row_sum = call(
        first_dual_kernel, [((2 * slots, 128), BF16)] + [vector] * 3, to_site(out), key, dual0, weight, pixel0
    )
    (out,) = call(pull_kernel, [((n_pix, 128), F32)], to_pix(out), *cov, scratch=[pltpu.VMEM((2 * slots, 128), F32)])
    out, site2 = call(push_kernel, [half_message, line], to_pix(out), price, site1, column_sum, *cov)
    (out,) = call(spread_kernel, [((n_site, 32, 128), F32)], to_pix(out), key)
    dual2, pixel2 = call(dual_kernel, [vector] * 2, to_site(out), row_sum, dual1, weight, pixel1)
    return site2.reshape(-1), pixel2.reshape(-1), dual2.reshape(-1)


def solution(mesh):
    placed = (
        P("pix", None, "site"),
        P("pix", "site"),
        P("site"),
        P(),
        P("site"),
        P("pix"),
        P("site"),
        P("pix"),
        P("pix"),
    )
    return jax.shard_map(
        functools.partial(local, mesh.shape["pix"], mesh.shape["site"]),
        mesh=mesh,
        in_specs=placed,
        out_specs=(P("site"), P("pix"), P("pix")),
        check_vma=False,
    )
```

```python
import functools

import jax
import jax.numpy as jnp
from jax import lax
from jax.experimental import pallas as pl
from jax.experimental.pallas import tpu as pltpu
from jax.sharding import PartitionSpec as P

F32 = jnp.float32
BF16 = jnp.bfloat16
HALF_SCALE = 2.0 ** (-10)
VMEM = pl.BlockSpec(memory_space=pltpu.VMEM)
HBM = pl.BlockSpec(memory_space=pltpu.HBM)


def iota(shape, dim):
    return lax.broadcasted_iota(jnp.int32, shape, dim)


def dot(a, b, dims=((1,), (0,))):
    return lax.dot_general(a, b, (dims, ((), ())), preferred_element_type=F32)


def exact_pick(onehot, values, dims):
    high = values.astype(BF16)
    rest = values - high.astype(F32)
    middle = rest.astype(BF16)
    low = (rest - middle.astype(F32)).astype(BF16)
    return dot(onehot, high, dims) + (dot(onehot, middle, dims) + dot(onehot, low, dims))


def call(body, outs, *args, scratch=(), specs=None, flops=0, nbytes=0, mib=8):
    return pl.pallas_call(
        body,
        out_shape=[jax.ShapeDtypeStruct(*o) for o in outs],
        in_specs=specs or [VMEM] * len(args),
        out_specs=[VMEM] * len(outs),
        scratch_shapes=list(scratch),
        cost_estimate=pl.CostEstimate(flops=flops, transcendentals=0, bytes_accessed=nbytes),
        compiler_params=pltpu.CompilerParams(vmem_limit_bytes=mib * 1024 * 1024),
    )(*args)


def in_hbm(value):
    return pltpu.with_memory_space_constraint(value, pltpu.HBM)


AHEAD = 6
SITE_ORDER = (6, 4, 0, 2, 5, 7, 1, 3)


def peer(j):
    chip = ((j >> 1) + 10) & 15
    y, x = chip >> 2, chip & 3
    return 8 * y + 2 * (x ^ (3 * (y & 1))) + (j & 1)


def fetch(m_hbm, buf, sems, first, last):
    copies = []
    for c, j in enumerate(range(first, last, 2)):
        part = (m_hbm.at[pl.ds(2 * peer(j), 4)], buf.at[pl.ds(2 * (j - first), 4)])
        copies.append(pltpu.make_async_copy(*part, sems.at[c]))
    for copy in copies[:AHEAD]:
        copy.start()
    return copies


def arrive(copies, c):
    copies[c].wait()
    for copy in copies[c + AHEAD : c + AHEAD + 1]:
        copy.start()


def build(buf, out_ref, half_gain, t):
    def pair(n, carry):
        gain = half_gain[...]
        level = jnp.concatenate([buf[2 * n + i].astype(F32) * HALF_SCALE + gain for i in range(2)], axis=1)
        out_ref[n] = (jnp.tanh(level) + 1.0).astype(BF16)
        return carry

    pair(t, 0)
    pair(t + 1, 0)


def build_kernel(
    m_hbm,
    pos_hbm,
    ids_hbm,
    gain_hbm,
    near_ref,
    map_ref,
    note_ref,
    half_gain,
    buf,
    pos_ref,
    ids_ref,
    gain_ref,
    sems,
    small_sems,
):
    small = [(pos_hbm, pos_ref), (ids_hbm, ids_ref), (gain_hbm, gain_ref)]
    small = [pltpu.make_async_copy(src, dst, small_sems.at[n]) for n, (src, dst) in enumerate(small)]
    for copy in small:
        copy.start()
    copies = fetch(m_hbm, buf, sems, 0, near_ref.shape[0])
    for copy in small:
        copy.wait()
    slots = m_hbm.shape[0]
    patterns = gain_ref.shape[0]
    onehot = (ids_ref[...] == iota((patterns, 128), 0)).astype(BF16)
    half_gain[...] = 0.5 * gain_pick(gain_ref[...], onehot)
    wide = jnp.broadcast_to(pos_ref[...].astype(F32), (128, slots)).astype(BF16)
    slot, row = iota((4 * slots, slots), 1), iota((4 * slots, slots), 0)
    map_ref[...] = dot((slot == 2 * peer(row >> 3) + ((row >> 1) & 1)).astype(BF16), wide, ((1,), (1,)))
    slot, row = iota((2 * slots, slots), 1), iota((2 * slots, slots), 0)
    note_ref[...] = dot((slot == 2 * peer(row >> 2) + (row & 1)).astype(BF16), wide, ((1,), (1,)))
    for c in range(len(copies)):
        arrive(copies, c)
        build(buf, near_ref, half_gain, 2 * c)


def gain_pick(gain, onehot):
    dims = ((0,), (0,))
    high = gain.astype(BF16)
    rest = gain - high.astype(F32)
    middle = rest.astype(BF16)
    low = (rest - middle.astype(F32)).astype(BF16)
    return dot(high, onehot, dims) + (dot(middle, onehot, dims) + dot(low, onehot, dims))


def tiles(*refs):
    return [ref.at[t] for ref in refs for t in range(ref.shape[0])]


def pull(rows, cov):
    total = 0.0
    for x, tile in zip(rows, cov):
        first = (iota(x.shape, 0) & 1) == 0
        left = jnp.concatenate([jnp.where(first, x, 0.0), jnp.where(first, 0.0, x)], axis=1)
        total = total + dot(left.astype(BF16), tile[...])
    return total


def own_columns(total, kind):
    rows = total[4 * kind : 4 * kind + 4]
    own = jnp.where(iota((4, 128), 0) < 2, rows[:, :128], rows[:, 128:])
    return jnp.sum(own, axis=0, keepdims=True)


def push(row, plain, cov, out_ref):
    spot = iota((8, 128), 0)
    value = jnp.broadcast_to(0.5 * row, (8, 128))
    if plain:
        value = jnp.where(spot < 4, 0.5, value)
    own = (spot & 2) == 0
    left = jnp.concatenate([jnp.where(own, value, 0.0), jnp.where(own, 0.0, value)], axis=1).astype(BF16)
    first = (spot & 1) == 0
    for t, tile in enumerate(cov):
        product = dot(left, tile[...], ((1,), (1,)))
        rows = jnp.where(first, product[:, :128], product[:, 128:])
        if plain:
            out_ref[t * 8 : (t + 1) * 8, :] = rows
        else:
            out_ref[t * 4 : t * 4 + 4, :] = rows[:4]


def first_pull_kernel(ag_ref, map_ref, note_ref, half_gain, near_ref, m_hbm, out_ref, far_ref, pick_ref, buf, sems):
    rows = map_ref.shape[0]
    near, pairs = near_ref.shape[0], ag_ref.shape[0]
    copies = fetch(m_hbm, buf, sems, near, pairs)
    marks = map_ref[...]
    row = iota((rows, 128), 0)
    key = jnp.where((marks >= 0.0) & ((row & 4) == 0), marks * 2.0 + (row & 1).astype(F32), -1.0)
    pick_ref[...] = (iota((rows, 128), 1).astype(F32) == key).astype(F32)
    plain = iota((8, 128), 0) >= 4

    def message_rows(t):
        part = slice(t * 8, (t + 1) * 8)
        picked = dot(pick_ref[part, :32].astype(BF16), ag_ref[t])
        return jnp.where(plain, (map_ref[part, :] >= 0.0).astype(F32), picked)

    total = pull([message_rows(t) for t in range(near)], tiles(near_ref))
    late = [message_rows(t) for t in range(near, pairs)]
    far = tiles(far_ref)
    for c in range(len(copies)):
        arrive(copies, c)
        build(buf, far_ref, half_gain, 2 * c)
        part = slice(2 * c, 2 * c + 2)
        total = total + pull(late[part], far[part])
    sums, pulled = own_columns(total, 1), own_columns(total, 0)
    place = iota(out_ref.shape, 0) & 3
    out_ref[...] = jnp.where(place == 0, sums, jnp.where(place == 1, pulled, note_ref[...]))


def first_push_kernel(in_ref, price_ref, site_ref, near_ref, far_ref, out_ref, new_ref, sum_ref):
    totals = jnp.sum(in_ref[...].reshape(-1, 8, 128), axis=0)
    column_sum = totals[0:1] + totals[4:5]
    pulled = totals[1:2] + totals[5:6]
    new = jnp.clip(site_ref[...] - (price_ref[...] - pulled / column_sum), 0.0, 1.0)
    new_ref[...] = new
    sum_ref[...] = column_sum
    push(2.0 * new - site_ref[...], True, tiles(near_ref, far_ref), out_ref)


def first_spread_kernel(x_ref, note_ref, out_ref, key_ref):
    notes = note_ref[...].astype(BF16)
    peers = notes.shape[0]

    def positions(rows, shift):
        row, column = iota((rows, peers), 0), iota((rows, peers), 1)
        return dot((column == 4 * (row >> shift) + 2 + ((row >> 1) & 1)).astype(BF16), notes)

    rows = x_ref.shape[0]
    row = iota((rows, 128), 0)
    marks = positions(rows, 3)
    key = jnp.where(marks >= 0.0, ((row >> 2) & 1).astype(F32) * 32.0 + marks * 2.0 + (row & 1).astype(F32), -1.0)
    onehot = (iota((rows, 128), 1).astype(F32) == key).astype(BF16)[:, :64]
    spread = exact_pick(onehot, x_ref[...], ((0,), (0,)))
    for s in range(out_ref.shape[0]):
        out_ref[s] = spread
    row = iota(key_ref.shape, 0)
    marks = positions(key_ref.shape[0], 2)
    key_ref[...] = jnp.where(marks >= 0.0, marks * 2.0 + (row & 1).astype(F32), -1.0)


def chooser(key_ref):
    return (iota(key_ref.shape, 1).astype(F32) == key_ref[...]).astype(BF16)[:, :32]


def step(pixel, dual, weight, pushed, row_sum):
    new = jnp.clip(pixel - (dual - weight), 0.0, 1.0)
    return new, jnp.maximum(dual + ((2.0 * new - pixel) - pushed) / (row_sum + 1.0), 0.0)


def first_dual_kernel(in_ref, key_ref, dual_ref, weight_ref, pixel_ref, out_ref, new_dual_ref, new_pixel_ref, row_ref):
    totals = jnp.sum(in_ref[...], axis=0)
    row_sum = totals[:32]
    row_ref[...] = row_sum
    new_pixel, new_dual = step(pixel_ref[...], dual_ref[...], weight_ref[...], totals[32:], row_sum)
    new_pixel_ref[...] = new_pixel
    new_dual_ref[...] = new_dual
    out_ref[...] = dot(chooser(key_ref), new_dual.astype(BF16)).astype(BF16)


def pull_kernel(x_ref, near_ref, far_ref, out_ref, rows_ref):
    cov = tiles(near_ref, far_ref)
    rows_ref[...] = x_ref[...].astype(F32)
    total = pull([rows_ref[t * 4 : (t + 1) * 4, :] for t in range(len(cov))], cov)
    out_ref[...] = jnp.broadcast_to(own_columns(total, 0), out_ref.shape)


def push_kernel(in_ref, price_ref, site_ref, sum_ref, near_ref, far_ref, out_ref, new_ref):
    pulled = jnp.sum(in_ref[...], axis=0, keepdims=True)
    new = jnp.clip(site_ref[...] - (price_ref[...] - pulled / sum_ref[...]), 0.0, 1.0)
    new_ref[...] = new
    push(2.0 * new - site_ref[...], False, tiles(near_ref, far_ref), out_ref)


def spread_kernel(x_ref, key_ref, out_ref):
    spread = exact_pick(chooser(key_ref), x_ref[...], ((0,), (0,)))
    for s in range(out_ref.shape[0]):
        out_ref[s] = spread


def dual_kernel(in_ref, row_ref, dual_ref, weight_ref, pixel_ref, new_dual_ref, new_pixel_ref):
    pushed = jnp.sum(in_ref[...], axis=0)
    new_pixel_ref[...], new_dual_ref[...] = step(
        pixel_ref[...], dual_ref[...], weight_ref[...], pushed, row_ref[...]
    )


def local(
    n_pix,
    n_site,
    margins,
    block_pos,
    pattern_ids,
    pattern_gain,
    site_price,
    weights,
    site_start,
    pixel_start,
    dual_start,
):
    slots = margins.shape[0]
    rows = 4 * slots
    pix_order = [[peer(j) for j in range(n_pix)]]

    def to_pix(x):
        x = x.reshape(n_pix, -1, 128)
        return lax.all_to_all(x, "pix", 0, 0, tiled=True, axis_index_groups=pix_order).reshape(-1, 128)

    def to_site(x):
        return lax.all_to_all(x, "site", 0, 0, tiled=True, axis_index_groups=[SITE_ORDER])

    price, site0 = site_price.reshape(1, 128), site_start.reshape(1, 128)
    dual0, weight, pixel0 = (v.reshape(32, 128) for v in (dual_start, weights, pixel_start))

    pairs, near = slots // 2, slots * 11 // 32 // 2 * 2
    far = pairs - near
    spot = iota((n_pix, 32, 128), 0) + iota((n_pix, 32, 128), 1) + iota((n_pix, 32, 128), 2)
    copies = jnp.where(spot < n_pix * 4096, dual0[None], 0.0).astype(BF16)
    gathered = to_pix(copies).reshape(n_pix, 32, 128)
    near_tiles, marks, notes, half_gain = call(
        build_kernel,
        [((near, 256, 256), BF16), ((4 * slots, 128), F32), ((2 * slots, 128), F32), ((256, 128), F32)],
        *(in_hbm(v) for v in (margins, block_pos.reshape(1, slots), pattern_ids.reshape(1, 128), pattern_gain)),
        scratch=[
            pltpu.VMEM((2 * near, 256, 128), jnp.int32),
            pltpu.VMEM((1, slots), jnp.int32),
            pltpu.VMEM((1, 128), jnp.int32),
            pltpu.VMEM(pattern_gain.shape, F32),
            pltpu.SemaphoreType.DMA((near // 2,)),
            pltpu.SemaphoreType.DMA((3,)),
        ],
        specs=[HBM] * 4,
        flops=10 * margins.size,
        nbytes=6 * margins.size,
        mib=16,
    )
    message, half_message, line, vector = [((n, 128), F32) for n in (4 * slots, 2 * slots, 1, 32)]
    out, far_tiles = call(
        first_pull_kernel,
        [half_message, ((far, 256, 256), BF16)],
        gathered,
        marks,
        notes,
        half_gain,
        near_tiles,
        in_hbm(margins),
        scratch=[
            pltpu.VMEM((4 * slots, 128), F32),
            pltpu.VMEM((2 * far, 256, 128), jnp.int32),
            pltpu.SemaphoreType.DMA((far // 2,)),
        ],
        specs=[VMEM] * 5 + [HBM],
    )
    cov = (near_tiles, far_tiles)
    summed = to_pix(out)
    out, site1, column_sum = call(first_push_kernel, [message, line, line], summed, price, site0, *cov)
    out, key = call(first_spread_kernel, [((n_site, 64, 128), F32), half_message], to_pix(out), summed)
    out, dual1, pixel1, row_sum = call(
        first_dual_kernel, [((2 * slots, 128), BF16)] + [vector] * 3, to_site(out), key, dual0, weight, pixel0
    )
    (out,) = call(pull_kernel, [((n_pix, 128), F32)], to_pix(out), *cov, scratch=[pltpu.VMEM((2 * slots, 128), F32)])
    out, site2 = call(push_kernel, [half_message, line], to_pix(out), price, site1, column_sum, *cov)
    (out,) = call(spread_kernel, [((n_site, 32, 128), F32)], to_pix(out), key)
    dual2, pixel2 = call(dual_kernel, [vector] * 2, to_site(out), row_sum, dual1, weight, pixel1)
    return site2.reshape(-1), pixel2.reshape(-1), dual2.reshape(-1)


def solution(mesh):
    placed = (
        P("pix", None, "site"),
        P("pix", "site"),
        P("site"),
        P(),
        P("site"),
        P("pix"),
        P("site"),
        P("pix"),
        P("pix"),
    )
    return jax.shard_map(
        functools.partial(local, mesh.shape["pix"], mesh.shape["site"]),
        mesh=mesh,
        in_specs=placed,
        out_specs=(P("site"), P("pix"), P("pix")),
        check_vma=False,
    )
```

```python
import functools

import jax
import jax.numpy as jnp
from jax import lax
from jax.experimental import pallas as pl
from jax.experimental.pallas import tpu as pltpu
from jax.sharding import PartitionSpec as P

F32 = jnp.float32
BF16 = jnp.bfloat16
HALF_SCALE = 2.0 ** (-10)
VMEM = pl.BlockSpec(memory_space=pltpu.VMEM)
HBM = pl.BlockSpec(memory_space=pltpu.HBM)


def iota(shape, dim):
    return lax.broadcasted_iota(jnp.int32, shape, dim)


def dot(a, b, dims=((1,), (0,))):
    return lax.dot_general(a, b, (dims, ((), ())), preferred_element_type=F32)


def exact_pick(onehot, values, dims):
    high = values.astype(BF16)
    rest = values - high.astype(F32)
    middle = rest.astype(BF16)
    low = (rest - middle.astype(F32)).astype(BF16)
    return dot(onehot, high, dims) + (dot(onehot, middle, dims) + dot(onehot, low, dims))


def call(body, outs, *args, scratch=(), specs=None, flops=0, nbytes=0, mib=8):
    return pl.pallas_call(
        body,
        out_shape=[jax.ShapeDtypeStruct(*o) for o in outs],
        in_specs=specs or [VMEM] * len(args),
        out_specs=[VMEM] * len(outs),
        scratch_shapes=list(scratch),
        cost_estimate=pl.CostEstimate(flops=flops, transcendentals=0, bytes_accessed=nbytes),
        compiler_params=pltpu.CompilerParams(vmem_limit_bytes=mib * 1024 * 1024),
    )(*args)


def in_hbm(value):
    return pltpu.with_memory_space_constraint(value, pltpu.HBM)


AHEAD = 6
SITE_ORDER = (6, 4, 0, 2, 5, 7, 1, 3)


def peer(j):
    chip = ((j >> 1) + 10) & 15
    y, x = chip >> 2, chip & 3
    return 8 * y + 2 * (x ^ (3 * (y & 1))) + ((j & 1) ^ 1)


def fetch(m_hbm, buf, sems, first, last):
    copies = []
    for c, j in enumerate(range(first, last, 2)):
        part = (m_hbm.at[pl.ds(2 * peer(j + 1), 4)], buf.at[pl.ds(2 * (j - first), 4)])
        copies.append(pltpu.make_async_copy(*part, sems.at[c]))
    for copy in copies[:AHEAD]:
        copy.start()
    return copies


def arrive(copies, c):
    copies[c].wait()
    for copy in copies[c + AHEAD : c + AHEAD + 1]:
        copy.start()


def build(buf, out_ref, half_gain, t):
    def pair(n, carry):
        gain = half_gain[...]
        level = jnp.concatenate([buf[2 * (n ^ 1) + i].astype(F32) * HALF_SCALE + gain for i in range(2)], axis=1)
        out_ref[n] = (jnp.tanh(level) + 1.0).astype(BF16)
        return carry

    pair(t, 0)
    pair(t + 1, 0)


def build_kernel(
    m_hbm,
    pos_hbm,
    ids_hbm,
    gain_hbm,
    near_ref,
    map_ref,
    note_ref,
    half_gain,
    buf,
    pos_ref,
    ids_ref,
    gain_ref,
    sems,
    small_sems,
):
    small = [(pos_hbm, pos_ref), (ids_hbm, ids_ref), (gain_hbm, gain_ref)]
    small = [pltpu.make_async_copy(src, dst, small_sems.at[n]) for n, (src, dst) in enumerate(small)]
    for copy in small:
        copy.start()
    copies = fetch(m_hbm, buf, sems, 0, near_ref.shape[0])
    for copy in small:
        copy.wait()
    slots = m_hbm.shape[0]
    patterns = gain_ref.shape[0]
    onehot = (ids_ref[...] == iota((patterns, 128), 0)).astype(BF16)
    half_gain[...] = 0.5 * gain_pick(gain_ref[...], onehot)
    wide = jnp.broadcast_to(pos_ref[...].astype(F32), (128, slots)).astype(BF16)
    slot, row = iota((4 * slots, slots), 1), iota((4 * slots, slots), 0)
    map_ref[...] = dot((slot == 2 * peer(row >> 3) + ((row >> 1) & 1)).astype(BF16), wide, ((1,), (1,)))
    slot, row = iota((2 * slots, slots), 1), iota((2 * slots, slots), 0)
    note_ref[...] = dot((slot == 2 * peer(row >> 2) + (row & 1)).astype(BF16), wide, ((1,), (1,)))
    for c in range(len(copies)):
        arrive(copies, c)
        build(buf, near_ref, half_gain, 2 * c)


def gain_pick(gain, onehot):
    dims = ((0,), (0,))
    high = gain.astype(BF16)
    rest = gain - high.astype(F32)
    middle = rest.astype(BF16)
    low = (rest - middle.astype(F32)).astype(BF16)
    return dot(high, onehot, dims) + (dot(middle, onehot, dims) + dot(low, onehot, dims))


def tiles(*refs):
    return [ref.at[t] for ref in refs for t in range(ref.shape[0])]


def pull(rows, cov):
    total = 0.0
    for x, tile in zip(rows, cov):
        first = (iota(x.shape, 0) & 1) == 0
        left = jnp.concatenate([jnp.where(first, x, 0.0), jnp.where(first, 0.0, x)], axis=1)
        total = total + dot(left.astype(BF16), tile[...])
    return total


def own_columns(total, kind):
    rows = total[4 * kind : 4 * kind + 4]
    own = jnp.where(iota((4, 128), 0) < 2, rows[:, :128], rows[:, 128:])
    return jnp.sum(own, axis=0, keepdims=True)


def push(row, plain, cov, out_ref):
    spot = iota((8, 128), 0)
    value = jnp.broadcast_to(0.5 * row, (8, 128))
    if plain:
        value = jnp.where(spot < 4, 0.5, value)
    own = (spot & 2) == 0
    left = jnp.concatenate([jnp.where(own, value, 0.0), jnp.where(own, 0.0, value)], axis=1).astype(BF16)
    first = (spot & 1) == 0
    for t, tile in enumerate(cov):
        product = dot(left, tile[...], ((1,), (1,)))
        rows = jnp.where(first, product[:, :128], product[:, 128:])
        if plain:
            out_ref[t * 8 : (t + 1) * 8, :] = rows
        else:
            out_ref[t * 4 : t * 4 + 4, :] = rows[:4]


def first_pull_kernel(ag_ref, map_ref, note_ref, half_gain, near_ref, m_hbm, out_ref, far_ref, pick_ref, buf, sems):
    rows = map_ref.shape[0]
    near, pairs = near_ref.shape[0], ag_ref.shape[0]
    copies = fetch(m_hbm, buf, sems, near, pairs)
    marks = map_ref[...]
    row = iota((rows, 128), 0)
    key = jnp.where((marks >= 0.0) & ((row & 4) == 0), marks * 2.0 + (row & 1).astype(F32), -1.0)
    pick_ref[...] = (iota((rows, 128), 1).astype(F32) == key).astype(F32)
    plain = iota((8, 128), 0) >= 4

    def message_rows(t):
        part = slice(t * 8, (t + 1) * 8)
        picked = dot(pick_ref[part, :32].astype(BF16), ag_ref[t])
        return jnp.where(plain, (map_ref[part, :] >= 0.0).astype(F32), picked)

    total = pull([message_rows(t) for t in range(near)], tiles(near_ref))
    late = [message_rows(t) for t in range(near, pairs)]
    far = tiles(far_ref)
    for c in range(len(copies)):
        arrive(copies, c)
        build(buf, far_ref, half_gain, 2 * c)
        part = slice(2 * c, 2 * c + 2)
        total = total + pull(late[part], far[part])
    sums, pulled = own_columns(total, 1), own_columns(total, 0)
    place = iota(out_ref.shape, 0) & 3
    out_ref[...] = jnp.where(place == 0, sums, jnp.where(place == 1, pulled, note_ref[...]))


def first_push_kernel(in_ref, price_ref, site_ref, near_ref, far_ref, out_ref, new_ref, sum_ref):
    totals = jnp.sum(in_ref[...].reshape(-1, 8, 128), axis=0)
    column_sum = totals[0:1] + totals[4:5]
    pulled = totals[1:2] + totals[5:6]
    new = jnp.clip(site_ref[...] - (price_ref[...] - pulled / column_sum), 0.0, 1.0)
    new_ref[...] = new
    sum_ref[...] = column_sum
    push(2.0 * new - site_ref[...], True, tiles(near_ref, far_ref), out_ref)


def first_spread_kernel(x_ref, note_ref, out_ref, key_ref):
    notes = note_ref[...].astype(BF16)
    peers = notes.shape[0]

    def positions(rows, shift):
        row, column = iota((rows, peers), 0), iota((rows, peers), 1)
        return dot((column == 4 * (row >> shift) + 2 + ((row >> 1) & 1)).astype(BF16), notes)

    rows = x_ref.shape[0]
    row = iota((rows, 128), 0)
    marks = positions(rows, 3)
    key = jnp.where(marks >= 0.0, ((row >> 2) & 1).astype(F32) * 32.0 + marks * 2.0 + (row & 1).astype(F32), -1.0)
    onehot = (iota((rows, 128), 1).astype(F32) == key).astype(BF16)[:, :64]
    spread = exact_pick(onehot, x_ref[...], ((0,), (0,)))
    for s in range(out_ref.shape[0]):
        out_ref[s] = spread
    row = iota(key_ref.shape, 0)
    marks = positions(key_ref.shape[0], 2)
    key_ref[...] = jnp.where(marks >= 0.0, marks * 2.0 + (row & 1).astype(F32), -1.0)


def chooser(key_ref):
    return (iota(key_ref.shape, 1).astype(F32) == key_ref[...]).astype(BF16)[:, :32]


def step(pixel, dual, weight, pushed, row_sum):
    new = jnp.clip(pixel - (dual - weight), 0.0, 1.0)
    return new, jnp.maximum(dual + ((2.0 * new - pixel) - pushed) / (row_sum + 1.0), 0.0)


def first_dual_kernel(in_ref, key_ref, dual_ref, weight_ref, pixel_ref, out_ref, new_dual_ref, new_pixel_ref, row_ref):
    totals = jnp.sum(in_ref[...], axis=0)
    row_sum = totals[:32]
    row_ref[...] = row_sum
    new_pixel, new_dual = step(pixel_ref[...], dual_ref[...], weight_ref[...], totals[32:], row_sum)
    new_pixel_ref[...] = new_pixel
    new_dual_ref[...] = new_dual
    out_ref[...] = dot(chooser(key_ref), new_dual.astype(BF16)).astype(BF16)


def pull_kernel(x_ref, near_ref, far_ref, out_ref, rows_ref):
    cov = tiles(near_ref, far_ref)
    rows_ref[...] = x_ref[...].astype(F32)
    total = pull([rows_ref[t * 4 : (t + 1) * 4, :] for t in range(len(cov))], cov)
    out_ref[...] = jnp.broadcast_to(own_columns(total, 0), out_ref.shape)


def push_kernel(in_ref, price_ref, site_ref, sum_ref, near_ref, far_ref, out_ref, new_ref):
    pulled = jnp.sum(in_ref[...], axis=0, keepdims=True)
    new = jnp.clip(site_ref[...] - (price_ref[...] - pulled / sum_ref[...]), 0.0, 1.0)
    new_ref[...] = new
    push(2.0 * new - site_ref[...], False, tiles(near_ref, far_ref), out_ref)


def spread_kernel(x_ref, key_ref, out_ref):
    spread = exact_pick(chooser(key_ref), x_ref[...], ((0,), (0,)))
    for s in range(out_ref.shape[0]):
        out_ref[s] = spread


def dual_kernel(in_ref, row_ref, dual_ref, weight_ref, pixel_ref, new_dual_ref, new_pixel_ref):
    pushed = jnp.sum(in_ref[...], axis=0)
    new_pixel_ref[...], new_dual_ref[...] = step(
        pixel_ref[...], dual_ref[...], weight_ref[...], pushed, row_ref[...]
    )


def local(
    n_pix,
    n_site,
    margins,
    block_pos,
    pattern_ids,
    pattern_gain,
    site_price,
    weights,
    site_start,
    pixel_start,
    dual_start,
):
    slots = margins.shape[0]
    rows = 4 * slots
    pix_order = [[peer(j) for j in range(n_pix)]]

    def to_pix(x):
        x = x.reshape(n_pix, -1, 128)
        return lax.all_to_all(x, "pix", 0, 0, tiled=True, axis_index_groups=pix_order).reshape(-1, 128)

    def to_site(x):
        return lax.all_to_all(x, "site", 0, 0, tiled=True, axis_index_groups=[SITE_ORDER])

    price, site0 = site_price.reshape(1, 128), site_start.reshape(1, 128)
    dual0, weight, pixel0 = (v.reshape(32, 128) for v in (dual_start, weights, pixel_start))

    pairs, near = slots // 2, slots * 11 // 32 // 2 * 2
    far = pairs - near
    spot = iota((n_pix, 32, 128), 0) + iota((n_pix, 32, 128), 1) + iota((n_pix, 32, 128), 2)
    copies = jnp.where(spot < n_pix * 4096, dual0[None], 0.0).astype(BF16)
    gathered = to_pix(copies).reshape(n_pix, 32, 128)
    near_tiles, marks, notes, half_gain = call(
        build_kernel,
        [((near, 256, 256), BF16), ((4 * slots, 128), F32), ((2 * slots, 128), F32), ((256, 128), F32)],
        *(in_hbm(v) for v in (margins, block_pos.reshape(1, slots), pattern_ids.reshape(1, 128), pattern_gain)),
        scratch=[
            pltpu.VMEM((2 * near, 256, 128), jnp.int32),
            pltpu.VMEM((1, slots), jnp.int32),
            pltpu.VMEM((1, 128), jnp.int32),
            pltpu.VMEM(pattern_gain.shape, F32),
            pltpu.SemaphoreType.DMA((near // 2,)),
            pltpu.SemaphoreType.DMA((3,)),
        ],
        specs=[HBM] * 4,
        flops=10 * margins.size,
        nbytes=6 * margins.size,
        mib=16,
    )
    message, half_message, line, vector = [((n, 128), F32) for n in (4 * slots, 2 * slots, 1, 32)]
    out, far_tiles = call(
        first_pull_kernel,
        [half_message, ((far, 256, 256), BF16)],
        gathered,
        marks,
        notes,
        half_gain,
        near_tiles,
        in_hbm(margins),
        scratch=[
            pltpu.VMEM((4 * slots, 128), F32),
            pltpu.VMEM((2 * far, 256, 128), jnp.int32),
            pltpu.SemaphoreType.DMA((far // 2,)),
        ],
        specs=[VMEM] * 5 + [HBM],
    )
    cov = (near_tiles, far_tiles)
    summed = to_pix(out)
    out, site1, column_sum = call(first_push_kernel, [message, line, line], summed, price, site0, *cov)
    out, key = call(first_spread_kernel, [((n_site, 64, 128), F32), half_message], to_pix(out), summed)
    out, dual1, pixel1, row_sum = call(
        first_dual_kernel, [((2 * slots, 128), BF16)] + [vector] * 3, to_site(out), key, dual0, weight, pixel0
    )
    (out,) = call(pull_kernel, [((n_pix, 128), F32)], to_pix(out), *cov, scratch=[pltpu.VMEM((2 * slots, 128), F32)])
    out, site2 = call(push_kernel, [half_message, line], to_pix(out), price, site1, column_sum, *cov)
    (out,) = call(spread_kernel, [((n_site, 32, 128), F32)], to_pix(out), key)
    dual2, pixel2 = call(dual_kernel, [vector] * 2, to_site(out), row_sum, dual1, weight, pixel1)
    return site2.reshape(-1), pixel2.reshape(-1), dual2.reshape(-1)


def solution(mesh):
    placed = (
        P("pix", None, "site"),
        P("pix", "site"),
        P("site"),
        P(),
        P("site"),
        P("pix"),
        P("site"),
        P("pix"),
        P("pix"),
    )
    return jax.shard_map(
        functools.partial(local, mesh.shape["pix"], mesh.shape["site"]),
        mesh=mesh,
        in_specs=placed,
        out_specs=(P("site"), P("pix"), P("pix")),
        check_vma=False,
    )
```
